32 devices in a mesh: dp: 8 (over z, x), tensor: 4 (over y, core).
Axes of the slice: x: 2, y: 2, z: 4, core: 2. Of those that a mesh axis runs over, the one named last changes fastest.
Arguments:
- tokens: bfloat16 [8192, 1536], P(('dp', 'tensor')), may hold values from -6 to 6
- cotangent: bfloat16 [8192, 1536], P(('dp', 'tensor')), may hold values from -6 to 6
- w_in: bfloat16 [1536, 4, 1536], P('dp', None, 'tensor'), may hold values from -0.21875 to 0.21875
- w_beta: bfloat16 [1536, 12], P('dp', 'tensor'), may hold values from -0.15625 to 0.15625
- beta_bias: float32 [12], replicated, may hold values from -3 to 3
- kernel: float32 [4, 1536], replicated, may hold values from -3 to 3
- w_out: bfloat16 [1536, 1536], P('tensor', 'dp'), may hold values from -0.4375 to 0.4375
- gain_attn: float32 [1536], replicated, may hold values from 0.5 to 1.5
- gain_ffn: float32 [1536], replicated, may hold values from 0.5 to 1.5
- w_gate: bfloat16 [1536, 4096], P('dp', 'tensor'), may hold values from -0.15625 to 0.15625
- w_up: bfloat16 [1536, 4096], P('dp', 'tensor'), may hold values from -0.15625 to 0.15625
- w_down: bfloat16 [4096, 1536], P('tensor', 'dp'), may hold values from -0.1875 to 0.1875
- lengths: int32 [24], replicated, may hold values from 0 to 1024, as said below
- offsets: int32 [24], replicated, may hold values from 0 to 8192, as said below
- permutation: int32 [8192], P(('dp', 'tensor')), may hold values from 0 to 8191, as said below
- inverse: int32 [8192], P(('dp', 'tensor')), may hold values from 0 to 8191, as said below
Outputs:
- output: bfloat16 [8192, 1536], P(('dp', 'tensor'))
- input_grad: bfloat16 [8192, 1536], P(('dp', 'tensor'))
- grad_w_in: float32 [1536, 4, 1536], P('dp', None, 'tensor')
- grad_w_beta: float32 [1536, 12], P('dp', 'tensor')
- grad_beta_bias: float32 [12], replicated
- grad_kernel: float32 [4, 1536], replicated
- grad_w_out: float32 [1536, 1536], P('tensor', 'dp')
- grad_gain_attn: float32 [1536], replicated
- grad_gain_ffn: float32 [1536], replicated
- grad_w_gate: float32 [1536, 4096], P('dp', 'tensor')
- grad_w_up: float32 [1536, 4096], P('dp', 'tensor')
- grad_w_down: float32 [4096, 1536], P('tensor', 'dp')
The draws below stay inside these ranges and needn't reach their ends.
Inputs may be any that keep to these rules, and one draw needn't show every extreme that they name: `lengths`: each slot of 1024 dealt positions holds up to three sequences packed from its start, the slot's three entries in order; an unused entry has length 0; the rest of a slot is padding; some sequence has exactly 1024 tokens. offsets of a slot's entries are the slot's first position plus the lengths before them. A permutation of the 8192 rows; the 256 dealt rows of each device take the same number of rows from every device's block of 256 input rows. inverse[permutation[p]] = p.
All inputs are finite; a program needn't handle non-finite values.
Results may differ from the reference program's by a relative error of at most 0.015.
The reference program's roundings to bfloat16 on the way count: a program that leaves them out, or rounds other values in their place, can miss the bound.
Values may be sent and summed in bfloat16 or wider, within the bound.
No kernel may reach another device: no remote copies, remote signals or barrier semaphores. Data moves between devices by JAX's collectives and lax.ppermute only.
A program may use at most 192 MiB of HBM per device.

```python
import jax
import jax.numpy as jnp
from jax import lax

D = 1536
H = 12
HEAD = 128
FF = 4096
KSIZE = 4
SLOT = 1024
TOK_DEV = 256
HD = 1536
TOKENS = 8192


def slot_tables(key):
    slot_count = TOKENS // SLOT
    base_key = jax.random.fold_in(key, 11)
    key_count, key_pad, key_cut = jax.random.split(base_key, 3)
    counts = jax.random.randint(key_count, (slot_count,), 1, 4)
    padding = jax.random.randint(key_pad, (slot_count,), 0, SLOT // 4 + 1)
    first_slot = jnp.arange(slot_count) == 0
    counts = jnp.where(first_slot, 1, counts)
    padding = jnp.where(first_slot, 0, padding)
    used_rows = SLOT - padding
    cut_points = jax.random.randint(key_cut, (slot_count, 2), 1, used_rows[:, None])
    cut_low = jnp.min(cut_points, axis=1)
    cut_high = jnp.max(cut_points, axis=1)
    first_len = jnp.where(counts == 1, used_rows, cut_low)
    second_len = jnp.where(counts == 1, 0, jnp.where(counts == 2, used_rows - cut_low, cut_high - cut_low))
    third_len = jnp.where(counts == 3, used_rows - cut_high, 0)
    lengths = jnp.stack([first_len, second_len, third_len], axis=1)
    zeros_col = jnp.zeros_like(first_len)
    starts = jnp.stack([zeros_col, first_len, first_len + second_len], axis=1) + (jnp.arange(slot_count) * SLOT)[:, None]
    return (lengths.reshape(-1).astype(jnp.int32), starts.reshape(-1).astype(jnp.int32))


def dealing(key):
    devs_all = TOKENS // TOK_DEV
    per_peer = TOK_DEV // devs_all
    base_key = jax.random.fold_in(key, 23)
    key_dest, key_source = jax.random.split(base_key)
    ramp = jnp.arange(TOK_DEV, dtype=jnp.int32)
    dest_order = jnp.argsort(jax.random.randint(key_dest, (devs_all, TOK_DEV), 0, 1 << 16) * TOK_DEV + ramp[None, :], axis=1)
    source_order = jnp.argsort(jax.random.randint(key_source, (devs_all, TOK_DEV), 0, 1 << 16) * TOK_DEV + ramp[None, :], axis=1)
    source = dest_order // per_peer
    within = dest_order % per_peer
    dest_index = jnp.arange(devs_all, dtype=jnp.int32)[:, None]
    column = dest_index * per_peer + within
    input_row = source * TOK_DEV + source_order[source, column]
    permutation = input_row.reshape(-1).astype(jnp.int32)
    inverse = jnp.zeros((TOKENS,), jnp.int32).at[permutation].set(jnp.arange(TOKENS, dtype=jnp.int32))
    return (permutation, inverse)


def draw_lengths(key, part):
    return slot_tables(key)[0]


def draw_offsets(key, part):
    return slot_tables(key)[1]


def draw_permutation(key, part):
    return dealing(key)[0]


def draw_inverse(key, part):
    return dealing(key)[1]


def block_scale(own_key, extent, pieces, least, largest):
    loudness, own = 1.0, jax.random.fold_in(own_key, 6)
    for position, parts in pieces:
        draws = jnp.exp(jax.random.uniform(jax.random.fold_in(own, position), (parts,), jnp.float32, least / len(pieces), largest / len(pieces)))
        loudness = loudness * jnp.repeat(draws, extent[position] // parts).reshape([-1 if axis == position else 1 for axis in range(len(extent))])
    return loudness


def centred(key, extent, spread, bound, cuts=(), held_as=jnp.bfloat16):
    drawn = jax.random.normal(key, extent, jnp.float32) * spread
    if len(cuts) > 0:
        drawn = block_scale(key, extent, cuts, -0.22, 0.18) * drawn
    return jnp.clip(drawn, min=-bound, max=bound).astype(held_as)


def setup_inputs(seed: int = 0) -> dict:
    streams_of = jax.random.split(jax.random.key(seed), 17)
    return {
        "tokens": centred(streams_of[0], (TOKENS, D), 1.0, 6.0, ((0, 32),)),
        "cotangent": centred(streams_of[1], (TOKENS, D), 1.0, 6.0, ((0, 32),)),
        "w_in": centred(streams_of[2], (D, 4, HD), (D // 2) ** -0.5, 0.21875, ((0, 8), (2, 4))),
        "w_beta": centred(streams_of[3], (D, H), D ** -0.5, 0.15625, ((0, 8), (1, 4))),
        "beta_bias": centred(streams_of[4], (H,), 1.0, 3.0, (), jnp.float32),
        "kernel": centred(streams_of[5], (KSIZE, HD), 0.5, 3.0, (), jnp.float32),
        "w_out": centred(streams_of[6], (HD, D), (HD // 8) ** -0.5, 0.4375, ((0, 4), (1, 8))),
        "gain_attn": jnp.clip(1.0 + 0.1 * jax.random.normal(streams_of[7], (D,), jnp.float32), 0.5, 1.5),
        "gain_ffn": jnp.clip(1.0 + 0.1 * jax.random.normal(streams_of[8], (D,), jnp.float32), 0.5, 1.5),
        "w_gate": centred(streams_of[9], (D, FF), D ** -0.5, 0.15625, ((0, 8), (1, 4))),
        "w_up": centred(streams_of[10], (D, FF), D ** -0.5, 0.15625, ((0, 8), (1, 4))),
        "w_down": centred(streams_of[11], (FF, D), (FF // 4) ** -0.5, 0.1875, ((0, 4), (1, 8))),
        "lengths": draw_lengths(jax.random.fold_in(streams_of[16], 71), 0),
        "offsets": draw_offsets(jax.random.fold_in(streams_of[16], 71), 0),
        "permutation": draw_permutation(jax.random.fold_in(streams_of[16], 71), 0),
        "inverse": draw_inverse(jax.random.fold_in(streams_of[16], 71), 0),
    }


eps_norm = 1e-06
eps_unit = 1e-06
highest = lax.Precision.HIGHEST

@jax.custom_vjp
def low(v):
    return lax.optimization_barrier(v.astype(jnp.bfloat16)).astype(jnp.float32)

@jax.custom_vjp
def low_back(v):
    return v

def low_keep(v):
    return (low(v), None)

def low_pass(kept, grad):
    return (grad,)

def back_keep(v):
    return (v, None)

def back_low(kept, grad):
    return (low(grad),)
low.defvjp(low_keep, low_pass)
low_back.defvjp(back_keep, back_low)

def seg_ids(positions, lengths, offsets):
    inside = (positions[:, None] >= offsets[None, :]) & (positions[:, None] < offsets[None, :] + lengths[None, :])
    number = jnp.arange(1, offsets.shape[0] + 1, dtype=jnp.int32)
    return (lax.optimization_barrier(jnp.sum(jnp.where(inside, number[None, :], 0), axis=1)) - 1).astype(jnp.int32)

def path_head(queries, keyed, valued, w_raw, beta_logit, kernel, segment):
    length = queries.shape[0]
    indices = jnp.arange(length, dtype=jnp.int32)
    same_seq = (segment[:, None] == segment[None, :]) & (segment[:, None] >= 0)
    diagonal = indices[:, None] == indices[None, :]
    is_later = indices[:, None] > indices[None, :]
    strict = is_later & same_seq
    inclusive = (is_later | diagonal) & same_seq
    allowed = inclusive | diagonal
    mixed_taps = w_raw * kernel[0][None, :]
    for tap_index in range(1, kernel.shape[0]):
        moved = jnp.concatenate([jnp.zeros((tap_index, w_raw.shape[1]), w_raw.dtype), w_raw[:-tap_index]], axis=0)
        linked = jnp.concatenate([jnp.zeros((tap_index,), bool), (segment[tap_index:] == segment[:-tap_index]) & (segment[tap_index:] >= 0)])
        mixed_taps = mixed_taps + jnp.where(linked[:, None], moved, 0.0) * kernel[tap_index][None, :]
    unit_dirs = mixed_taps * lax.rsqrt(lax.optimization_barrier(jnp.sum(mixed_taps * mixed_taps, axis=1, keepdims=True)) + eps_unit)
    beta_gain = 2.0 * jax.nn.sigmoid(beta_logit)
    lower_part = jnp.where(strict, jnp.dot(unit_dirs, unit_dirs.T, precision=highest), 0.0) * beta_gain[None, :]
    right_side = jnp.where(inclusive, jnp.dot(queries, unit_dirs.T, precision=highest), 0.0) * beta_gain[None, :]
    coeffs = jax.scipy.linalg.solve_triangular(lower_part, right_side.T, trans=1, lower=True, unit_diagonal=True).T
    dir_keys = jnp.where(strict, jnp.dot(unit_dirs, keyed.T, precision=highest), 0.0)
    scores = jnp.dot(queries, keyed.T, precision=highest) - jnp.dot(coeffs, dir_keys, precision=highest)
    scores = jnp.where(allowed, scores * queries.shape[1] ** (-0.5), -1e+30)
    top_score = lax.optimization_barrier(jnp.max(scores, axis=1, keepdims=True))
    weights = jnp.exp(scores - top_score)
    probability = weights / lax.optimization_barrier(jnp.sum(weights, axis=1, keepdims=True))
    return jnp.dot(probability, valued, precision=highest)

def path_attention(queries, keyed, valued, w_raw, beta_logit, kernel, segment, slot_len):
    row_count, head_count, head_width = queries.shape
    slot_count = row_count // slot_len
    taps = kernel.shape[0]

    def to_items(array):
        return array.reshape(slot_count, slot_len, head_count, head_width).transpose(0, 2, 1, 3).reshape(slot_count * head_count, slot_len, head_width)
    blocks = (to_items(queries), to_items(keyed), to_items(valued), to_items(w_raw), beta_logit.reshape(slot_count, slot_len, head_count).transpose(0, 2, 1).reshape(slot_count * head_count, slot_len), jnp.broadcast_to(kernel.reshape(taps, head_count, head_width).transpose(1, 0, 2)[None], (slot_count, head_count, taps, head_width)).reshape(slot_count * head_count, taps, head_width), jnp.broadcast_to(segment.reshape(slot_count, 1, slot_len), (slot_count, head_count, slot_len)).reshape(slot_count * head_count, slot_len))
    results = lax.map(lambda member: jax.checkpoint(path_head)(*member), blocks)
    return results.reshape(slot_count, head_count, slot_len, head_width).transpose(0, 2, 1, 3).reshape(row_count, head_count, head_width)

def rms(values, gain_vec):
    return values * lax.rsqrt(lax.optimization_barrier(jnp.mean(values * values, axis=1, keepdims=True)) + eps_norm) * gain_vec[None, :]

def block_forward(inputs, w_in, w_beta, beta_bias, kernel, w_out, gain_attn, gain_ffn, w_gate, w_up, w_down, permutation, inverse, segment):
    dealt_rows = inputs[permutation]
    normed = low(rms(dealt_rows, gain_attn))
    projected = low_back(jnp.dot(normed, w_in.reshape(D, 4 * HD), precision=highest)).reshape(TOKENS, 4, H, HEAD)
    queries = low(projected[:, 0])
    keyed = low(projected[:, 1])
    valued = low(projected[:, 2])
    w_raw = projected[:, 3]
    beta_logit = low_back(jnp.dot(normed, w_beta, precision=highest)) + beta_bias[None, :]
    attended = low(path_attention(queries, keyed, valued, w_raw, beta_logit, kernel, segment, SLOT)).reshape(TOKENS, HD)
    branch = low_back(jnp.dot(attended, w_out, precision=highest))
    middle = dealt_rows + branch
    normed2 = low(rms(middle, gain_ffn))
    gate_value = low_back(jnp.dot(normed2, w_gate, precision=highest))
    up_value = low_back(jnp.dot(normed2, w_up, precision=highest))
    hidden = low(jax.nn.silu(gate_value) * up_value)
    ffn_out = low_back(jnp.dot(hidden, w_down, precision=highest))
    return (middle + ffn_out)[inverse]

def reference(tokens, cotangent, w_in, w_beta, beta_bias, kernel, w_out, gain_attn, gain_ffn, w_gate, w_up, w_down, lengths, offsets, permutation, inverse):
    segment = seg_ids(jnp.arange(TOKENS, dtype=jnp.int32), lengths, offsets)
    floats = tuple((array.astype(jnp.float32) for array in (tokens, w_in, w_beta, beta_bias, kernel, w_out, gain_attn, gain_ffn, w_gate, w_up, w_down)))

    def forward(*values):
        return block_forward(*values, permutation, inverse, segment)
    output, pullback = jax.vjp(forward, *floats)
    gradients = pullback(cotangent.astype(jnp.float32))
    return (output.astype(jnp.bfloat16), gradients[0].astype(jnp.bfloat16), gradients[1], gradients[2], gradients[3], gradients[4], gradients[5], gradients[6], gradients[7], gradients[8], gradients[9], gradients[10])
```

```python
import functools
import jax
import jax.numpy as jnp
from jax import lax
from jax.experimental import pallas as pl
from jax.experimental.pallas import tpu as pltpu
from jax.sharding import PartitionSpec as P

SLOT = 1024
eps_norm = 1e-06

BLK = 128
HEADW = 128
eps_unit = 1e-06
f32, bf16 = jnp.float32, jnp.bfloat16
NN = (((1,), (0,)), ((), ()))
NT = (((1,), (1,)), ((), ()))
TN = (((0,), (0,)), ((), ()))


def bdims(dims):
    (a, b), _ = dims
    return ((tuple(i + 1 for i in a), tuple(i + 1 for i in b)), ((0,), (0,)))


def dot1(a, b, dims):
    return lax.dot_general(a, b, dims if a.ndim == 2 else bdims(dims), preferred_element_type=f32)


def split(x):
    hi = x.astype(bf16)
    return hi, (x - hi.astype(f32)).astype(bf16)


def dot3(a, b, dims):
    return dot1(a[0], b[0], dims) + (dot1(a[0], b[1], dims) + dot1(a[1], b[0], dims))


def iota2(rows, cols):
    r = lax.broadcasted_iota(jnp.int32, (rows, cols), 0)
    c = lax.broadcasted_iota(jnp.int32, (rows, cols), 1)
    return r, c


def convolve(w, taps, link):
    mixed = w * taps[0:1]
    for t in range(1, taps.shape[0]):
        mixed = mixed + (pltpu.roll(w, t, 0) * link[:, t : t + 1]) * taps[t : t + 1]
    return mixed


def unit_inverse(low, r, c):
    same8 = ((r // 8) == (c // 8))[None]
    n1 = jnp.where(same8, low, 0.0)
    s1 = split(n1)
    n2 = dot3(s1, s1, NN)
    s2 = split(n2)
    n4 = dot3(s2, s2, NN)
    x = jnp.where(r == c, 1.0, 0.0)[None] - n1
    x = x + dot3(split(x), s2, NN)
    x = x + dot3(split(x), split(n4), NN)
    size = 8
    while size < BLK:
        level = (((r // (2 * size)) == (c // (2 * size))) & ((r // size) != (c // size)))[None]
        part = jnp.where(level, low, 0.0)
        sx = split(x)
        x = x - dot3(split(dot3(sx, split(part), NN)), sx, NN)
        size *= 2
    return x


def pick_logit(tail_ref, bias_ref, head):
    lane = lax.broadcasted_iota(jnp.int32, (1, tail_ref.shape[1]), 1)
    return jnp.sum(jnp.where(lane == head, tail_ref[...] + bias_ref[...], 0.0), axis=1, keepdims=True)


def fwd_body(q_ref, k_ref, v_ref, w_ref, tail_ref, bias_ref, tap_ref, link_ref, segc_ref, segr_ref,
             o_ref, lse_ref, u_ref, gram_ref, tinv_ref, tr_ref, qt_ref, p_ref, sd_ref, hist_ref,
             kct, bl, *, group):
    length = q_ref.shape[0]
    blocks = length // BLK
    bl[...] = pick_logit(tail_ref, bias_ref, pl.program_id(0))
    mixed = convolve(w_ref[...], tap_ref[...], link_ref[...])
    inv = lax.rsqrt(jnp.sum(mixed * mixed, axis=1, keepdims=True) + eps_unit)
    u_ref[0] = mixed * inv
    r, c = iota2(BLK, BLK)

    def phase1(g, _):
        rows = pl.ds(pl.multiple_of(g * group * BLK, BLK), group * BLK)
        three = lambda x: x.reshape(group, BLK, x.shape[-1])
        u = three(u_ref[0, rows, :])
        qb = three(q_ref[rows, :]).astype(bf16)
        kb = three(k_ref[rows, :]).astype(bf16)
        beta = three(2.0 * jax.nn.sigmoid(bl[rows, :]))
        sc = three(segc_ref[rows, :])
        sr = segr_ref[pl.ds(g * group, group)]
        same = sc == sr
        strict = same & (r > c)[None]
        upper = same & (r <= c)[None]
        u2 = split(u)
        uk = dot1(u2[0], kb, NT) + dot1(u2[1], kb, NT)
        uq = dot1(u2[0], qb, NT) + dot1(u2[1], qb, NT)
        s = jnp.where(strict, dot3(u2, u2, NT), 0.0)
        w = jnp.where(strict, uk, 0.0)
        rqt = jnp.where(upper, uq, 0.0)
        blk = pl.ds(g * group, group)
        gram_ref[0, blk, :, 0:BLK] = s
        gram_ref[0, blk, :, BLK : 2 * BLK] = rqt
        gram_ref[0, blk, :, 2 * BLK :] = w
        tinv = unit_inverse(beta * s, r, c)
        tinv_ref[0, blk] = tinv
        t2 = split(tinv)
        tr_u = dot3(t2, split(beta * u), NN)
        tr_w = dot3(t2, split(beta * w), NN)
        tr_ref[0, blk, :, 0:BLK] = tr_u
        tr_ref[0, blk, :, BLK:] = tr_w
        rq2 = split(rqt)
        tru2, trw2 = split(tr_u), split(tr_w)
        qt_ref[0, blk] = (qb.astype(f32) - dot3(rq2, tru2, TN)).astype(bf16)
        sd_ref[0, blk] = dot1(qb, kb, NT) - dot3(rq2, trw2, TN)
        p_ref[0, blk] = (jnp.where(r == c, 1.0, 0.0)[None] - dot3(u2, tru2, TN)).astype(bf16)
        kt = dot3(u2, trw2, TN)
        for i in range(group):
            kct[g * group + i] = (kb[i].astype(f32).T - kt[i]).astype(bf16)
        return 0

    lax.fori_loop(0, blocks // group, phase1, 0)
    scale = HEADW ** -0.5
    base = 0
    hist = None
    for b in range(blocks):
        n = b * BLK
        rows = pl.ds(n, BLK)
        same = segc_ref[rows, :] == segr_ref[b]
        diag = jnp.where(same & (r >= c), sd_ref[0, b] * scale, -1e30)
        top = jnp.max(diag, axis=1, keepdims=True)
        if b:
            off = dot1(qt_ref[0, b], hist_ref[0, :, pl.ds(base, n)], NN) * scale
            pieces = []
            for j in range(b):
                link = segc_ref[rows, :] == segr_ref[j]
                pieces.append(jnp.where(link, off[:, j * BLK : (j + 1) * BLK], -1e30))
            off = jnp.concatenate(pieces, axis=1)
            top = jnp.maximum(top, jnp.max(off, axis=1, keepdims=True))
            ed, eo = jnp.exp(diag - top), jnp.exp(off - top)
            total = jnp.sum(ed, axis=1, keepdims=True) + jnp.sum(eo, axis=1, keepdims=True)
            out = dot1(ed.astype(bf16), v_ref[rows, :].astype(bf16), NN) + dot1(
                eo.astype(bf16), v_ref[pl.ds(0, n), :].astype(bf16), NN)
        else:
            ed = jnp.exp(diag - top)
            total = jnp.sum(ed, axis=1, keepdims=True)
            out = dot1(ed.astype(bf16), v_ref[rows, :].astype(bf16), NN)
        o_ref[rows, :] = (out / total).astype(bf16)
        lse_ref[0, rows, :] = top + jnp.log(total)
        if b < blocks - 1:
            nxt = base + n
            if b:
                moved = dot1(p_ref[0, b], hist_ref[0, :, pl.ds(base, n)], NN)
                hist_ref[0, :, pl.ds(nxt, n)] = moved.astype(bf16)
            hist_ref[0, :, pl.ds(nxt + n, BLK)] = kct[b]
            base = nxt


def bwd_body(q_ref, k_ref, v_ref, w_ref, tail_ref, bias_ref, tap_ref, link_ref, segc_ref, segr_ref,
             lse_ref, u_ref, gram_ref, tinv_ref, tr_ref, qt_ref, p_ref, sd_ref, hist_ref, do_ref,
             dproj_ref, dbias_ref, dtap_ref,
             dkc, dvt, dz, du, bl, *, group, do_heads):
    length = q_ref.shape[0]
    blocks = length // BLK
    head = pl.program_id(0)
    heads = do_heads
    scale = HEADW ** -0.5
    r, c = iota2(BLK, BLK)
    bl[...] = pick_logit(tail_ref, bias_ref, head)
    lane = lax.broadcasted_iota(jnp.int32, (1, HEADW), 1)

    @pl.when(head == 0)
    def _():
        dproj_ref[:, 4 * heads * HEADW :] = jnp.zeros((length, HEADW), bf16)
        dbias_ref[...] = jnp.zeros_like(dbias_ref)

    dkc[...] = jnp.zeros_like(dkc)
    dvt[...] = jnp.zeros_like(dvt)
    base = sum(range(blocks - 1)) * BLK
    for b in reversed(range(blocks)):
        n = b * BLK
        rows = pl.ds(n, BLK)
        lse = lse_ref[0, rows, :]
        same = segc_ref[rows, :] == segr_ref[b]
        pd = jnp.exp(jnp.where(same & (r >= c), sd_ref[0, b] * scale, -1e30) - lse)
        do = do_ref[rows, :]
        dob = do.astype(bf16)
        dot_t = do.T.astype(bf16)
        dpd = dot1(dob, v_ref[rows, :].astype(bf16), NT)
        delta = jnp.sum(pd * dpd, axis=1, keepdims=True)
        if b:
            kc = hist_ref[0, :, pl.ds(base, n)]
            off = dot1(qt_ref[0, b], kc, NN) * scale - lse
            pieces = []
            for j in range(b):
                link = segc_ref[rows, :] == segr_ref[j]
                pieces.append(jnp.where(link, off[:, j * BLK : (j + 1) * BLK], -1e30))
            po = jnp.exp(jnp.concatenate(pieces, axis=1))
            dpo = dot1(dob, v_ref[pl.ds(0, n), :].astype(bf16), NT)
            delta = delta + jnp.sum(po * dpo, axis=1, keepdims=True)
            go = (po * (dpo - delta) * scale).astype(bf16)
            dvt[:, pl.ds(0, n)] += dot1(dot_t, po.astype(bf16), NN)
        dvt[:, rows] += dot1(dot_t, pd.astype(bf16), NN)
        dz[b, 0:BLK, BLK:] = pd * (dpd - delta) * scale
        dz[b, BLK:, BLK:] = dkc[:, rows]
        if b:
            dz[b, 0:BLK, 0:BLK] = dot1(go, kc, NT)
            old = dkc[:, pl.ds(0, n)].astype(bf16)
            dz[b, BLK:, 0:BLK] = dot1(old, kc, NT)
            qtt = qt_ref[0, b].astype(f32).T.astype(bf16)
            dkc[:, pl.ds(0, n)] = dot1(p_ref[0, b], old, TN) + dot1(qtt, go, NN)
            base -= (b - 1) * BLK
        else:
            dz[b, 0:BLK, 0:BLK] = jnp.zeros((BLK, BLK), f32)
            dz[b, BLK:, 0:BLK] = jnp.zeros((BLK, BLK), f32)

    feats = heads * HEADW
    col = lambda part: pl.ds(pl.multiple_of(part * feats + head * HEADW, HEADW), HEADW)

    def phase2(g, _):
        rows = pl.ds(pl.multiple_of(g * group * BLK, BLK), group * BLK)
        blk = pl.ds(g * group, group)
        three = lambda x: x.reshape(group, BLK, x.shape[-1])
        flat = lambda x: x.reshape(group * BLK, x.shape[-1])
        u = three(u_ref[0, rows, :])
        qb = three(q_ref[rows, :]).astype(bf16)
        kb = three(k_ref[rows, :]).astype(bf16)
        sig = three(jax.nn.sigmoid(bl[rows, :]))
        beta = 2.0 * sig
        same = three(segc_ref[rows, :]) == segr_ref[blk]
        strict = same & (r > c)[None]
        upper = same & (r <= c)[None]
        gram = gram_ref[0, blk]
        s, rqt, w = gram[:, :, :BLK], gram[:, :, BLK : 2 * BLK], gram[:, :, 2 * BLK :]
        t2 = split(tinv_ref[0, blk])
        tr = tr_ref[0, blk]
        tr2 = split(tr)
        z2 = split(dz[blk])
        left2 = split(jnp.concatenate([rqt, u], axis=2))
        lti2 = split(dot3(t2, left2, TN))
        yi = dot3(lti2, z2, NN)
        r2 = jnp.concatenate([u, w], axis=2) - dot1(s.astype(bf16), tr2[0], NN)
        dbeta = -jnp.sum(yi * r2, axis=2, keepdims=True)
        dlogit = jnp.where(lane == head, flat(dbeta * beta * (1.0 - sig)), 0.0)
        tail = pl.ds(4 * heads * HEADW, HEADW)
        dproj_ref[rows, tail] = jnp.where(lane == head, dlogit.astype(bf16), dproj_ref[rows, tail])
        dbias_ref[...] += jnp.sum(dlogit, axis=0, keepdims=True)
        y = beta * yi
        dlt = -dot3(tr2, z2, NT)
        ds = jnp.where(strict, dot3(split(y), tr2, NT), 0.0)
        drqt = jnp.where(upper, dlt[:, :, :BLK], 0.0)
        dw = jnp.where(strict, -y[:, :, BLK:], 0.0)
        ub = u.astype(bf16)
        drqb, dwb, dsb = drqt.astype(bf16), dw.astype(bf16), ds.astype(bf16)
        gd = dz[blk, 0:BLK, BLK:].astype(bf16)
        du[rows, :] = flat(
            dlt[:, :, BLK:] - y[:, :, :BLK] + dot1(drqb, qb, NN) + dot1(dwb, kb, NN)
            + dot1(dsb, ub, NN) + dot1(dsb, ub, TN))
        dq = dz[blk, 0:BLK, 0:BLK] + dot1(gd, kb, NN) + dot1(drqb, ub, TN)
        dproj_ref[rows, col(0)] = flat(dq).astype(bf16)
        dk = dot1(gd, qb, TN) + dot1(dwb, ub, TN)
        dkt = dz[blk, BLK:, BLK:]
        for i in range(group):
            here = pl.ds(pl.multiple_of((g * group + i) * BLK, BLK), BLK)
            dproj_ref[here, col(1)] = (dk[i] + dkt[i].T).astype(bf16)
            dproj_ref[here, col(2)] = dvt[:, here].T.astype(bf16)
        return 0

    lax.fori_loop(0, blocks // group, phase2, 0)
    taps, link, wv = tap_ref[...], link_ref[...], w_ref[...]
    mixed = convolve(wv, taps, link)
    inv = lax.rsqrt(jnp.sum(mixed * mixed, axis=1, keepdims=True) + eps_unit)
    duv = du[...]
    dm = inv * duv - mixed * ((inv * inv * inv) * jnp.sum(duv * mixed, axis=1, keepdims=True))
    dwr = dm * taps[0:1]
    dtap_ref[0:1, :] = jnp.sum(dm * wv, axis=0, keepdims=True)
    for t in range(1, taps.shape[0]):
        dml = dm * link[:, t : t + 1]
        dwr = dwr + pltpu.roll(dml, length - t, 0) * taps[t : t + 1]
        dtap_ref[t : t + 1, :] = jnp.sum(dml * pltpu.roll(wv, t, 0), axis=0, keepdims=True)
    dproj_ref[:, col(3)] = dwr.astype(bf16)


def attn_specs(length, heads, ntap):
    blocks = length // BLK
    part = lambda p: pl.BlockSpec((length, HEADW), lambda h: (0, p * heads + h))
    ins = [part(0), part(1), part(2), part(3),
           pl.BlockSpec((length, HEADW), lambda h: (0, 4 * heads)),
           pl.BlockSpec((1, HEADW), lambda h: (0, 0)),
           pl.BlockSpec((ntap, HEADW), lambda h: (0, h)),
           pl.BlockSpec((length, ntap), lambda h: (0, 0)),
           pl.BlockSpec((length, 1), lambda h: (0, 0)),
           pl.BlockSpec((blocks, 1, BLK), lambda h: (0, 0, 0))]
    tri = blocks * (blocks - 1) // 2 * BLK
    shapes = [((length, 1), f32), ((length, HEADW), f32), ((blocks, BLK, 3 * BLK), f32),
              ((blocks, BLK, BLK), f32), ((blocks, BLK, 2 * BLK), f32), ((blocks, BLK, BLK), bf16),
              ((blocks, BLK, BLK), bf16), ((blocks, BLK, BLK), f32), ((BLK, tri), bf16)]
    saved = [jax.ShapeDtypeStruct((heads,) + s, d) for s, d in shapes]
    saved_specs = [pl.BlockSpec((1,) + s, (lambda h: (h, 0, 0)) if len(s) == 2 else (lambda h: (h, 0, 0, 0)))
                   for s, _ in shapes]
    return ins, saved, saved_specs


def attn_fwd(proj, bias, taps, link, segc, segr, group=4):
    length, heads = proj.shape[0], taps.shape[1] // HEADW
    ins, saved, saved_specs = attn_specs(length, heads, taps.shape[0])
    return pl.pallas_call(
        functools.partial(fwd_body, group=group),
        grid=(heads,),
        in_specs=ins,
        out_specs=[pl.BlockSpec((length, HEADW), lambda h: (0, h))] + saved_specs,
        out_shape=[jax.ShapeDtypeStruct((length, heads * HEADW), bf16)] + saved,
        scratch_shapes=[pltpu.VMEM((length // BLK, BLK, BLK), bf16), pltpu.VMEM((length, 1), f32)],
        compiler_params=pltpu.CompilerParams(vmem_limit_bytes=56 << 20),
        cost_estimate=pl.CostEstimate(flops=12 * 10**9, bytes_accessed=40 << 20, transcendentals=10**6),
        name="path_fwd",
    )(proj, proj, proj, proj, proj, bias, taps, link, segc, segr)


def attn_bwd(proj, bias, taps, link, segc, segr, saved, d_att, group=4):
    length, heads = proj.shape[0], taps.shape[1] // HEADW
    ins, _, saved_specs = attn_specs(length, heads, taps.shape[0])
    blocks = length // BLK
    return pl.pallas_call(
        functools.partial(bwd_body, group=group, do_heads=heads),
        grid=(heads,),
        in_specs=ins + saved_specs + [pl.BlockSpec((length, HEADW), lambda h: (0, h))],
        out_specs=[pl.BlockSpec((length, (4 * heads + 1) * HEADW), lambda h: (0, 0)),
                   pl.BlockSpec((1, HEADW), lambda h: (0, 0)),
                   pl.BlockSpec((taps.shape[0], HEADW), lambda h: (0, h))],
        out_shape=[jax.ShapeDtypeStruct((length, (4 * heads + 1) * HEADW), bf16),
                   jax.ShapeDtypeStruct((1, HEADW), f32),
                   jax.ShapeDtypeStruct(taps.shape, f32)],
        scratch_shapes=[pltpu.VMEM((BLK, length), f32), pltpu.VMEM((BLK, length), f32),
                        pltpu.VMEM((blocks, 2 * BLK, 2 * BLK), f32), pltpu.VMEM((length, HEADW), f32), pltpu.VMEM((length, 1), f32)],
        compiler_params=pltpu.CompilerParams(vmem_limit_bytes=60 << 20),
        cost_estimate=pl.CostEstimate(flops=30 * 10**9, bytes_accessed=60 << 20, transcendentals=10**6),
        name="path_bwd",
    )(proj, proj, proj, proj, proj, bias, taps, link, segc, segr, *saved, d_att)


def attn_tables(segment, ntap):
    length = segment.shape[0]
    at = jnp.arange(length, dtype=jnp.int32)
    ids = jnp.where(segment >= 0, segment, -1 - at)
    link = [jnp.ones((length,), f32)]
    for t in range(1, ntap):
        same = jnp.concatenate([jnp.zeros((t,), bool), ids[t:] == ids[:-t]])
        link.append(same.astype(f32))
    return jnp.stack(link, axis=1), ids[:, None], ids.reshape(length // BLK, 1, BLK)


def seg_ids(positions, lengths, offsets):
    inside = (positions[:, None] >= offsets[None, :]) & (
        positions[:, None] < offsets[None, :] + lengths[None, :]
    )
    number = jnp.arange(1, offsets.shape[0] + 1, dtype=jnp.int32)
    return jnp.sum(jnp.where(inside, number[None, :], 0), axis=1) - 1


def rms_scale(values):
    return lax.rsqrt(jnp.mean(values * values, axis=1, keepdims=True) + eps_norm)


def rms_back(values, gain_vec, d_normed):
    inv_rms = rms_scale(values)
    scaled = d_normed * gain_vec[None, :]
    d_values = inv_rms * scaled - values * (inv_rms * inv_rms * inv_rms) * jnp.mean(
        scaled * values, axis=1, keepdims=True
    )
    d_gain = jnp.sum(d_normed * values * inv_rms, axis=0)
    return (d_values, d_gain)


def rank_of(keys):
    return jnp.sum((keys[None, :] < keys[:, None]).astype(jnp.int32), axis=1)


def pick_rows(choice, rows):
    return jnp.dot(choice.astype(bf16), rows, preferred_element_type=f32).astype(bf16)


def exchange(rows):
    return lax.all_to_all(rows, ("dp", "tensor"), split_axis=0, concat_axis=0, tiled=True)


def swap(rows, bit):
    size = lax.axis_size("tensor")
    return lax.ppermute(rows, "tensor", [(i, i ^ bit) for i in range(size)])


def gather_group(rows):
    half = jnp.concatenate([rows, swap(rows, 2)], axis=0)
    return jnp.concatenate([half, swap(half, 1)], axis=0)


def sum_group(terms):
    half = terms.shape[0] // 2
    near = terms[:half] + swap(terms[half:].astype(bf16), 1).astype(f32)
    return near[: half // 2] + swap(near[half // 2 :].astype(bf16), 2).astype(f32)


def to_slot(rows, me):
    size = rows.shape[0] // 4
    out = jnp.zeros_like(rows)
    for place, other in enumerate((0, 2, 1, 3)):
        piece = rows[place * size : (place + 1) * size]
        out = lax.dynamic_update_slice_in_dim(out, piece, (me ^ other) * size, axis=0)
    return out


def from_slot(rows, me):
    size = rows.shape[0] // 4
    return jnp.concatenate(
        [lax.dynamic_slice_in_dim(rows, (me ^ other) * size, size) for other in (0, 2, 1, 3)], axis=0
    )


def gather_weight(shard):
    return lax.all_gather(shard, "dp", axis=0, tiled=True)


def sum_weight(terms):
    return lax.psum_scatter(terms.astype(bf16), "dp", scatter_dimension=0, tiled=True).astype(f32)


def sum_all(part):
    return jnp.sum(lax.all_gather(part, ("dp", "tensor"), axis=0), axis=0)


def dot(a, b, dims=NN):
    return lax.dot_general(a, b, dims, preferred_element_type=f32)


def shards(
    tokens, cotangent, w_in, w_beta, beta_bias, kernel, w_out, gain_attn, gain_ffn,
    w_gate, w_up, w_down, lengths, offsets, permutation, inverse,
):
    row_count = tokens.shape[0]
    me = lax.axis_index("tensor")
    group_rows = row_count * lax.axis_size("tensor")
    assert group_rows == SLOT and lax.axis_size("tensor") == 4
    heads = w_beta.shape[1]
    feats = w_in.shape[2]
    hidden_units = w_gate.shape[1]
    shard_rows = w_in.shape[0]
    at = jnp.arange(row_count, dtype=jnp.int32)

    send = rank_of(inverse)[None, :] == at[:, None]
    place = rank_of((permutation // row_count) * row_count + at)[:, None] == at[None, :]
    dealt = pick_rows(place, exchange(pick_rows(send, tokens))).astype(f32)
    dealt_cot = pick_rows(place, exchange(pick_rows(send, cotangent)))

    narrow = jnp.pad(w_beta, ((0, 0), (0, HEADW - heads)))
    full_in = gather_weight(jnp.concatenate([w_in.reshape(shard_rows, 4 * feats), narrow], axis=1))
    full_out = gather_weight(w_out.T)
    full_wide = gather_weight(jnp.concatenate([w_gate, w_up], axis=1))
    full_down = gather_weight(w_down.T)

    positions = lax.axis_index("dp") * group_rows + jnp.arange(group_rows, dtype=jnp.int32)
    tables = attn_tables(seg_ids(positions, lengths, offsets), kernel.shape[0])
    bias_local = lax.dynamic_slice_in_dim(beta_bias, me * heads, heads)
    bias_row = jnp.pad(bias_local, (0, HEADW - heads))[None, :]
    taps = lax.dynamic_slice_in_dim(kernel, me * feats, feats, axis=1)

    normed = (dealt * rms_scale(dealt) * gain_attn[None, :]).astype(bf16)
    normed_all = to_slot(gather_group(normed), me)
    projected = dot(normed_all, full_in)
    attended, *saved = attn_fwd(projected, bias_row, taps, *tables)
    attended = from_slot(attended, me)
    branch = sum_group(dot(attended, full_out, NT))
    middle = dealt + branch
    normed2 = (middle * rms_scale(middle) * gain_ffn[None, :]).astype(bf16)
    ffn_rows = gather_group(normed2)
    wide = dot(ffn_rows, full_wide)
    gate_value, up_value = wide[:, :hidden_units], wide[:, hidden_units:]
    sig_gate = jax.nn.sigmoid(gate_value)
    hidden = (gate_value * sig_gate * up_value).astype(bf16)
    ffn_out = sum_group(dot(hidden, full_down, NT))
    output = (middle + ffn_out).astype(bf16)

    cot_rows = gather_group(dealt_cot)
    grad_down = dot(cot_rows, hidden, TN)
    d_hidden = dot(cot_rows, full_down)
    d_gate = d_hidden * up_value * sig_gate * (1.0 + gate_value * (1.0 - sig_gate))
    d_up = d_hidden * gate_value * sig_gate
    d_wide = jnp.concatenate([d_gate.astype(bf16), d_up.astype(bf16)], axis=1)
    grad_wide = dot(ffn_rows, d_wide, TN)
    d_normed2 = sum_group(dot(d_wide, full_wide, NT))
    d_from_ffn, d_gain_ffn = rms_back(middle, gain_ffn, d_normed2)
    d_middle = dealt_cot.astype(f32) + d_from_ffn
    branch_rows = gather_group(d_middle.astype(bf16))
    grad_out = dot(branch_rows, attended, TN)
    d_attended = to_slot(dot(branch_rows, full_out), me)
    d_projected, d_bias, d_taps = attn_bwd(projected, bias_row, taps, *tables, saved, d_attended)
    grad_in = dot(normed_all, d_projected, TN)
    d_normed = sum_group(dot(from_slot(d_projected, me), full_in, NT))
    d_first, d_gain_attn = rms_back(dealt, gain_attn, d_normed)
    d_input = (d_middle + d_first).astype(bf16)

    sum_down = sum_weight(grad_down).T
    sum_wide = sum_weight(grad_wide)
    sum_out = sum_weight(grad_out).T
    sum_in = sum_weight(grad_in)

    tap_terms = lax.dynamic_update_slice_in_dim(
        jnp.zeros(kernel.shape, f32), d_taps, me * feats, axis=1
    )
    bias_terms = lax.dynamic_update_slice_in_dim(
        jnp.zeros((1, kernel.shape[1]), f32), d_bias[:, :heads], me * heads, axis=1
    )
    small = sum_all(jnp.concatenate([tap_terms, bias_terms, d_gain_ffn[None, :]], axis=0))
    gain_attn_sum = sum_all(d_gain_attn[None, :])[0]
    tap_count = kernel.shape[0]

    back = rank_of(permutation)[None, :] == at[:, None]
    home = rank_of((inverse // row_count) * row_count + at)[:, None] == at[None, :]
    out_rows = pick_rows(home, exchange(pick_rows(back, output)))
    grad_rows = pick_rows(home, exchange(pick_rows(back, d_input)))
    return (
        out_rows,
        grad_rows,
        sum_in[:, : 4 * feats].reshape(shard_rows, 4, feats),
        sum_in[:, 4 * feats : 4 * feats + heads],
        small[tap_count, : beta_bias.shape[0]],
        small[:tap_count],
        sum_out,
        gain_attn_sum,
        small[tap_count + 1],
        sum_wide[:, :hidden_units],
        sum_wide[:, hidden_units:],
        sum_down,
    )


def solution(mesh):
    both, rows = P(("dp", "tensor")), P(("dp", "tensor"), None)
    in_specs = (
        rows, rows, P("dp", None, "tensor"), P("dp", "tensor"), P(), P(), P("tensor", "dp"), P(), P(),
        P("dp", "tensor"), P("dp", "tensor"), P("tensor", "dp"), P(), P(), both, both,
    )
    out_specs = (
        rows, rows, P("dp", None, "tensor"), P("dp", "tensor"), P(), P(), P("tensor", "dp"), P(), P(),
        P("dp", "tensor"), P("dp", "tensor"), P("tensor", "dp"),
    )
    return jax.shard_map(shards, mesh=mesh, in_specs=in_specs, out_specs=out_specs, check_vma=False)
```

```python
import functools
import jax
import jax.numpy as jnp
from jax import lax
from jax.experimental import pallas as pl
from jax.experimental.pallas import tpu as pltpu
from jax.sharding import Mesh, PartitionSpec as P

SLOT = 1024
eps_norm = 1e-06

BLK = 128
HEADW = 128
eps_unit = 1e-06
f32, bf16 = jnp.float32, jnp.bfloat16
NN = (((1,), (0,)), ((), ()))
NT = (((1,), (1,)), ((), ()))
TN = (((0,), (0,)), ((), ()))


def bdims(dims):
    (a, b), _ = dims
    return ((tuple(i + 1 for i in a), tuple(i + 1 for i in b)), ((0,), (0,)))


def dot1(a, b, dims):
    return lax.dot_general(a, b, dims if a.ndim == 2 else bdims(dims), preferred_element_type=f32)


def split(x):
    hi = x.astype(bf16)
    return hi, (x - hi.astype(f32)).astype(bf16)


def dot3(a, b, dims):
    return dot1(a[0], b[0], dims) + (dot1(a[0], b[1], dims) + dot1(a[1], b[0], dims))


def iota2(rows, cols):
    r = lax.broadcasted_iota(jnp.int32, (rows, cols), 0)
    c = lax.broadcasted_iota(jnp.int32, (rows, cols), 1)
    return r, c


def convolve(w, taps, link):
    mixed = w * taps[0:1]
    for t in range(1, taps.shape[0]):
        mixed = mixed + (pltpu.roll(w, t, 0) * link[:, t : t + 1]) * taps[t : t + 1]
    return mixed


def unit_inverse(low, r, c):
    same8 = ((r // 8) == (c // 8))[None]
    n1 = jnp.where(same8, low, 0.0)
    s1 = split(n1)
    n2 = dot3(s1, s1, NN)
    s2 = split(n2)
    n4 = dot3(s2, s2, NN)
    x = jnp.where(r == c, 1.0, 0.0)[None] - n1
    x = x + dot3(split(x), s2, NN)
    x = x + dot3(split(x), split(n4), NN)
    size = 8
    while size < BLK:
        level = (((r // (2 * size)) == (c // (2 * size))) & ((r // size) != (c // size)))[None]
        part = jnp.where(level, low, 0.0)
        sx = split(x)
        x = x - dot3(split(dot3(sx, split(part), NN)), sx, NN)
        size *= 2
    return x


def pick_logit(tail_ref, bias_ref, head):
    lane = lax.broadcasted_iota(jnp.int32, (1, tail_ref.shape[1]), 1)
    return jnp.sum(jnp.where(lane == head, tail_ref[...] + bias_ref[...], 0.0), axis=1, keepdims=True)


def fwd_body(q_ref, k_ref, v_ref, w_ref, tail_ref, bias_ref, tap_ref, link_ref, segc_ref, segr_ref,
             o_ref, lse_ref, u_ref, gram_ref, tinv_ref, tr_ref, qt_ref, p_ref, sd_ref, hist_ref,
             kct, bl, *, group, head):
    length = q_ref.shape[0]
    blocks = length // BLK
    bl[...] = pick_logit(tail_ref, bias_ref, head)
    mixed = convolve(w_ref[...], tap_ref[...], link_ref[...])
    inv = lax.rsqrt(jnp.sum(mixed * mixed, axis=1, keepdims=True) + eps_unit)
    u_ref[0] = mixed * inv
    r, c = iota2(BLK, BLK)

    def phase1(g, _):
        rows = pl.ds(pl.multiple_of(g * group * BLK, BLK), group * BLK)
        three = lambda x: x.reshape(group, BLK, x.shape[-1])
        u = three(u_ref[0, rows, :])
        qb = three(q_ref[rows, :]).astype(bf16)
        kb = three(k_ref[rows, :]).astype(bf16)
        beta = three(2.0 * jax.nn.sigmoid(bl[rows, :]))
        sc = three(segc_ref[rows, :])
        sr = segr_ref[pl.ds(g * group, group)]
        same = sc == sr
        strict = same & (r > c)[None]
        upper = same & (r <= c)[None]
        u2 = split(u)
        uk = dot1(u2[0], kb, NT) + dot1(u2[1], kb, NT)
        uq = dot1(u2[0], qb, NT) + dot1(u2[1], qb, NT)
        s = jnp.where(strict, dot3(u2, u2, NT), 0.0)
        w = jnp.where(strict, uk, 0.0)
        rqt = jnp.where(upper, uq, 0.0)
        blk = pl.ds(g * group, group)
        gram_ref[0, blk, :, 0:BLK] = s
        gram_ref[0, blk, :, BLK : 2 * BLK] = rqt
        gram_ref[0, blk, :, 2 * BLK :] = w
        tinv = unit_inverse(beta * s, r, c)
        tinv_ref[0, blk] = tinv
        t2 = split(tinv)
        tr_u = dot3(t2, split(beta * u), NN)
        tr_w = dot3(t2, split(beta * w), NN)
        tr_ref[0, blk, :, 0:BLK] = tr_u
        tr_ref[0, blk, :, BLK:] = tr_w
        rq2 = split(rqt)
        tru2, trw2 = split(tr_u), split(tr_w)
        qt_ref[0, blk] = (qb.astype(f32) - dot3(rq2, tru2, TN)).astype(bf16)
        sd_ref[0, blk] = dot1(qb, kb, NT) - dot3(rq2, trw2, TN)
        p_ref[0, blk] = (jnp.where(r == c, 1.0, 0.0)[None] - dot3(u2, tru2, TN)).astype(bf16)
        kt = dot3(u2, trw2, TN)
        for i in range(group):
            kct[g * group + i] = (kb[i].astype(f32).T - kt[i]).astype(bf16)
        return 0

    lax.fori_loop(0, blocks // group, phase1, 0)
    scale = HEADW ** -0.5
    base = 0
    hist = None
    for b in range(blocks):
        n = b * BLK
        rows = pl.ds(n, BLK)
        same = segc_ref[rows, :] == segr_ref[b]
        diag = jnp.where(same & (r >= c), sd_ref[0, b] * scale, -1e30)
        top = jnp.max(diag, axis=1, keepdims=True)
        if b:
            off = dot1(qt_ref[0, b], hist_ref[0, :, pl.ds(base, n)], NN) * scale
            pieces = []
            for j in range(b):
                link = segc_ref[rows, :] == segr_ref[j]
                pieces.append(jnp.where(link, off[:, j * BLK : (j + 1) * BLK], -1e30))
            off = jnp.concatenate(pieces, axis=1)
            top = jnp.maximum(top, jnp.max(off, axis=1, keepdims=True))
            ed, eo = jnp.exp(diag - top), jnp.exp(off - top)
            total = jnp.sum(ed, axis=1, keepdims=True) + jnp.sum(eo, axis=1, keepdims=True)
            out = dot1(ed.astype(bf16), v_ref[rows, :].astype(bf16), NN) + dot1(
                eo.astype(bf16), v_ref[pl.ds(0, n), :].astype(bf16), NN)
        else:
            ed = jnp.exp(diag - top)
            total = jnp.sum(ed, axis=1, keepdims=True)
            out = dot1(ed.astype(bf16), v_ref[rows, :].astype(bf16), NN)
        o_ref[rows, :] = (out / total).astype(bf16)
        lse_ref[0, rows, :] = top + jnp.log(total)
        if b < blocks - 1:
            nxt = base + n
            if b:
                moved = dot1(p_ref[0, b], hist_ref[0, :, pl.ds(base, n)], NN)
                hist_ref[0, :, pl.ds(nxt, n)] = moved.astype(bf16)
            hist_ref[0, :, pl.ds(nxt + n, BLK)] = kct[b]
            base = nxt


def bwd_body(q_ref, k_ref, v_ref, w_ref, tail_ref, bias_ref, tap_ref, link_ref, segc_ref, segr_ref,
             lse_ref, u_ref, gram_ref, tinv_ref, tr_ref, qt_ref, p_ref, sd_ref, hist_ref, do_ref,
             dproj_ref, dbias_ref, dtap_ref,
             dkc, dvt, dz, du, bl, *, group, heads):
    head = pl.program_id(0)
    length = q_ref.shape[0]
    blocks = length // BLK
    scale = HEADW ** -0.5
    r, c = iota2(BLK, BLK)
    bl[...] = pick_logit(tail_ref, bias_ref, head)
    lane = lax.broadcasted_iota(jnp.int32, (1, HEADW), 1)

    @pl.when(head == 0)
    def _():
        dproj_ref[:, 4 * heads * HEADW :] = jnp.zeros((length, HEADW), bf16)
        dbias_ref[...] = jnp.zeros_like(dbias_ref)

    dkc[...] = jnp.zeros_like(dkc)
    dvt[...] = jnp.zeros_like(dvt)
    base = sum(range(blocks - 1)) * BLK
    for b in reversed(range(blocks)):
        n = b * BLK
        rows = pl.ds(n, BLK)
        lse = lse_ref[0, rows, :]
        same = segc_ref[rows, :] == segr_ref[b]
        pd = jnp.exp(jnp.where(same & (r >= c), sd_ref[0, b] * scale, -1e30) - lse)
        do = do_ref[rows, :]
        dob = do.astype(bf16)
        dot_t = do.T.astype(bf16)
        dpd = dot1(dob, v_ref[rows, :].astype(bf16), NT)
        delta = jnp.sum(pd * dpd, axis=1, keepdims=True)
        if b:
            kc = hist_ref[0, :, pl.ds(base, n)]
            off = dot1(qt_ref[0, b], kc, NN) * scale - lse
            pieces = []
            for j in range(b):
                link = segc_ref[rows, :] == segr_ref[j]
                pieces.append(jnp.where(link, off[:, j * BLK : (j + 1) * BLK], -1e30))
            po = jnp.exp(jnp.concatenate(pieces, axis=1))
            dpo = dot1(dob, v_ref[pl.ds(0, n), :].astype(bf16), NT)
            delta = delta + jnp.sum(po * dpo, axis=1, keepdims=True)
            go = (po * (dpo - delta) * scale).astype(bf16)
            dvt[:, pl.ds(0, n)] += dot1(dot_t, po.astype(bf16), NN)
        dvt[:, rows] += dot1(dot_t, pd.astype(bf16), NN)
        dz[b, 0:BLK, BLK:] = pd * (dpd - delta) * scale
        dz[b, BLK:, BLK:] = dkc[:, rows]
        if b:
            dz[b, 0:BLK, 0:BLK] = dot1(go, kc, NT)
            old = dkc[:, pl.ds(0, n)].astype(bf16)
            dz[b, BLK:, 0:BLK] = dot1(old, kc, NT)
            qtt = qt_ref[0, b].astype(f32).T.astype(bf16)
            dkc[:, pl.ds(0, n)] = dot1(p_ref[0, b], old, TN) + dot1(qtt, go, NN)
            base -= (b - 1) * BLK
        else:
            dz[b, 0:BLK, 0:BLK] = jnp.zeros((BLK, BLK), f32)
            dz[b, BLK:, 0:BLK] = jnp.zeros((BLK, BLK), f32)

    col = lambda part: pl.ds(pl.multiple_of((4 * head + part) * HEADW, HEADW), HEADW)

    def phase2(g, _):
        rows = pl.ds(pl.multiple_of(g * group * BLK, BLK), group * BLK)
        blk = pl.ds(g * group, group)
        three = lambda x: x.reshape(group, BLK, x.shape[-1])
        flat = lambda x: x.reshape(group * BLK, x.shape[-1])
        u = three(u_ref[0, rows, :])
        qb = three(q_ref[rows, :]).astype(bf16)
        kb = three(k_ref[rows, :]).astype(bf16)
        sig = three(jax.nn.sigmoid(bl[rows, :]))
        beta = 2.0 * sig
        same = three(segc_ref[rows, :]) == segr_ref[blk]
        strict = same & (r > c)[None]
        upper = same & (r <= c)[None]
        gram = gram_ref[0, blk]
        s, rqt, w = gram[:, :, :BLK], gram[:, :, BLK : 2 * BLK], gram[:, :, 2 * BLK :]
        t2 = split(tinv_ref[0, blk])
        tr = tr_ref[0, blk]
        tr2 = split(tr)
        z2 = split(dz[blk])
        left2 = split(jnp.concatenate([rqt, u], axis=2))
        lti2 = split(dot3(t2, left2, TN))
        yi = dot3(lti2, z2, NN)
        r2 = jnp.concatenate([u, w], axis=2) - dot1(s.astype(bf16), tr2[0], NN)
        dbeta = -jnp.sum(yi * r2, axis=2, keepdims=True)
        dlogit = jnp.where(lane == head, flat(dbeta * beta * (1.0 - sig)), 0.0)
        tail = pl.ds(4 * heads * HEADW, HEADW)
        dproj_ref[rows, tail] = jnp.where(lane == head, dlogit.astype(bf16), dproj_ref[rows, tail])
        dbias_ref[...] += jnp.sum(dlogit, axis=0, keepdims=True)
        y = beta * yi
        dlt = -dot3(tr2, z2, NT)
        ds = jnp.where(strict, dot3(split(y), tr2, NT), 0.0)
        drqt = jnp.where(upper, dlt[:, :, :BLK], 0.0)
        dw = jnp.where(strict, -y[:, :, BLK:], 0.0)
        ub = u.astype(bf16)
        drqb, dwb, dsb = drqt.astype(bf16), dw.astype(bf16), ds.astype(bf16)
        gd = dz[blk, 0:BLK, BLK:].astype(bf16)
        du[rows, :] = flat(
            dlt[:, :, BLK:] - y[:, :, :BLK] + dot1(drqb, qb, NN) + dot1(dwb, kb, NN)
            + dot1(dsb, ub, NN) + dot1(dsb, ub, TN))
        dq = dz[blk, 0:BLK, 0:BLK] + dot1(gd, kb, NN) + dot1(drqb, ub, TN)
        dproj_ref[rows, col(0)] = flat(dq).astype(bf16)
        dk = dot1(gd, qb, TN) + dot1(dwb, ub, TN)
        dkt = dz[blk, BLK:, BLK:]
        for i in range(group):
            here = pl.ds(pl.multiple_of((g * group + i) * BLK, BLK), BLK)
            dproj_ref[here, col(1)] = (dk[i] + dkt[i].T).astype(bf16)
            dproj_ref[here, col(2)] = dvt[:, here].T.astype(bf16)
        return 0

    lax.fori_loop(0, blocks // group, phase2, 0)
    taps, link, wv = tap_ref[...], link_ref[...], w_ref[...]
    mixed = convolve(wv, taps, link)
    inv = lax.rsqrt(jnp.sum(mixed * mixed, axis=1, keepdims=True) + eps_unit)
    duv = du[...]
    dm = inv * duv - mixed * ((inv * inv * inv) * jnp.sum(duv * mixed, axis=1, keepdims=True))
    dwr = dm * taps[0:1]
    dtap_ref[0:1, :] = jnp.sum(dm * wv, axis=0, keepdims=True)
    for t in range(1, taps.shape[0]):
        dml = dm * link[:, t : t + 1]
        dwr = dwr + pltpu.roll(dml, length - t, 0) * taps[t : t + 1]
        dtap_ref[t : t + 1, :] = jnp.sum(dml * pltpu.roll(wv, t, 0), axis=0, keepdims=True)
    dproj_ref[:, col(3)] = dwr.astype(bf16)


def attn_specs(length, heads, head_of, ntap):
    blocks = length // BLK
    part = lambda p: pl.BlockSpec((length, HEADW), lambda i: (0, 4 * head_of(i) + p))
    ins = [part(0), part(1), part(2), part(3),
           pl.BlockSpec((length, HEADW), lambda i: (0, 4 * heads)),
           pl.BlockSpec((1, HEADW), lambda i: (0, 0)),
           pl.BlockSpec((ntap, HEADW), lambda i: (0, head_of(i))),
           pl.BlockSpec((length, ntap), lambda i: (0, 0)),
           pl.BlockSpec((length, 1), lambda i: (0, 0)),
           pl.BlockSpec((blocks, 1, BLK), lambda i: (0, 0, 0))]
    tri = blocks * (blocks - 1) // 2 * BLK
    shapes = [((length, 1), f32), ((length, HEADW), f32), ((blocks, BLK, 3 * BLK), f32),
              ((blocks, BLK, BLK), f32), ((blocks, BLK, 2 * BLK), f32), ((blocks, BLK, BLK), bf16),
              ((blocks, BLK, BLK), bf16), ((blocks, BLK, BLK), f32), ((BLK, tri), bf16)]
    saved = [jax.ShapeDtypeStruct((heads,) + s, d) for s, d in shapes]
    saved_specs = [
        pl.BlockSpec((1,) + s, (lambda i: (head_of(i), 0, 0)) if len(s) == 2 else (lambda i: (head_of(i), 0, 0, 0)))
        for s, _ in shapes
    ]
    return ins, saved, saved_specs


def attn_fwd(head, proj, bias, taps, link, segc, segr, before, group=4):
    length, heads = proj.shape[0], taps.shape[1] // HEADW
    ins, saved, saved_specs = attn_specs(length, heads, lambda i: head, taps.shape[0])
    out_specs = [pl.BlockSpec((length, HEADW), lambda i: (0, head))] + saved_specs
    out_shape = [jax.ShapeDtypeStruct((length, heads * HEADW), bf16)] + saved
    count = len(ins)

    def body(*refs):
        fwd_body(*refs[:count], *refs[count + len(before) :], group=group, head=head)

    return pl.pallas_call(
        body,
        grid=(1,),
        in_specs=ins + [pl.BlockSpec(memory_space=pl.ANY)] * len(before),
        out_specs=out_specs,
        out_shape=out_shape,
        input_output_aliases={count + i: i for i in range(len(before))},
        scratch_shapes=[pltpu.VMEM((length // BLK, BLK, BLK), bf16), pltpu.VMEM((length, 1), f32)],
        compiler_params=pltpu.CompilerParams(vmem_limit_bytes=58 << 20),
        cost_estimate=pl.CostEstimate(flops=4 * 10**9, bytes_accessed=1 << 20, transcendentals=10**6),
        name="path_fwd",
    )(proj, proj, proj, proj, proj, bias, taps, link, segc, segr, *before)


def attn_bwd(proj, bias, taps, link, segc, segr, saved, d_att, group=4):
    length, heads = proj.shape[0], taps.shape[1] // HEADW
    ins, _, saved_specs = attn_specs(length, heads, lambda i: i, taps.shape[0])
    blocks = length // BLK
    width = (4 * heads + 1) * HEADW
    return pl.pallas_call(
        functools.partial(bwd_body, group=group, heads=heads),
        grid=(heads,),
        in_specs=ins + saved_specs + [pl.BlockSpec((length, HEADW), lambda i: (0, i))],
        out_specs=[pl.BlockSpec((length, width), lambda i: (0, 0)),
                   pl.BlockSpec((1, HEADW), lambda i: (0, 0)),
                   pl.BlockSpec((taps.shape[0], HEADW), lambda i: (0, i))],
        out_shape=[jax.ShapeDtypeStruct((length, width), bf16),
                   jax.ShapeDtypeStruct((1, HEADW), f32),
                   jax.ShapeDtypeStruct(taps.shape, f32)],
        scratch_shapes=[pltpu.VMEM((BLK, length), f32), pltpu.VMEM((BLK, length), f32),
                        pltpu.VMEM((blocks, 2 * BLK, 2 * BLK), f32), pltpu.VMEM((length, HEADW), f32),
                        pltpu.VMEM((length, 1), f32)],
        compiler_params=pltpu.CompilerParams(vmem_limit_bytes=60 << 20),
        cost_estimate=pl.CostEstimate(flops=10**9, bytes_accessed=1 << 20, transcendentals=10**6),
        name="path_bwd",
    )(proj, proj, proj, proj, proj, bias, taps, link, segc, segr, *saved, d_att)


def place_body(shapes, columns, rows, at_ref, *refs):
    out, count = refs[len(shapes)], 0
    for source, shape, column in zip(refs, shapes, columns):
        for piece in [source] if len(shape) == 2 else [source.at[i] for i in range(shape[0])]:
            first = pl.multiple_of(at_ref[count] * rows, rows)
            out[pl.ds(first, rows), pl.ds(column, shape[-1])] = piece[...]
            count += 1


def place_rows(sources, places, columns=None, width=None):
    columns = columns or [0] * len(sources)
    width = width or sources[0].shape[-1]
    rows, kind = sources[0].shape[-2], sources[0].dtype
    total = sum(source.size for source in sources)
    size = 2 * total * kind.itemsize
    whole = lambda shape: pl.BlockSpec(shape, lambda i, at: (0,) * len(shape))
    return pl.pallas_call(
        functools.partial(place_body, [source.shape for source in sources], columns, rows),
        grid_spec=pltpu.PrefetchScalarGridSpec(
            num_scalar_prefetch=1,
            grid=(1,),
            in_specs=[whole(source.shape) for source in sources],
            out_specs=whole((total // width, width)),
        ),
        out_shape=jax.ShapeDtypeStruct((total // width, width), kind),
        compiler_params=pltpu.CompilerParams(vmem_limit_bytes=(2 * size) + (4 << 20)),
        cost_estimate=pl.CostEstimate(flops=0, bytes_accessed=size, transcendentals=0),
        name="place_rows",
    )(places, *sources)


def attn_tables(segment, ntap):
    length = segment.shape[0]
    at = jnp.arange(length, dtype=jnp.int32)
    ids = jnp.where(segment >= 0, segment, -1 - at)
    link = [jnp.ones((length,), f32)]
    for t in range(1, ntap):
        same = jnp.concatenate([jnp.zeros((t,), bool), ids[t:] == ids[:-t]])
        link.append(same.astype(f32))
    return jnp.stack(link, axis=1), ids[:, None], ids.reshape(length // BLK, 1, BLK)


def seg_ids(positions, lengths, offsets):
    inside = (positions[:, None] >= offsets[None, :]) & (
        positions[:, None] < offsets[None, :] + lengths[None, :]
    )
    number = jnp.arange(1, offsets.shape[0] + 1, dtype=jnp.int32)
    return jnp.sum(jnp.where(inside, number[None, :], 0), axis=1) - 1


def rms_scale(values):
    return lax.rsqrt(jnp.mean(values * values, axis=1, keepdims=True) + eps_norm)


def rms_back(values, gain_vec, d_normed):
    inv_rms = rms_scale(values)
    scaled = d_normed * gain_vec[None, :]
    d_values = inv_rms * scaled - values * (inv_rms * inv_rms * inv_rms) * jnp.mean(
        scaled * values, axis=1, keepdims=True
    )
    d_gain = jnp.sum(d_normed * values * inv_rms, axis=0)
    return (d_values, d_gain)


def rank_of(keys):
    return jnp.sum((keys[None, :] < keys[:, None]).astype(jnp.int32), axis=1)


def pick_rows(choice, rows):
    return jnp.dot(choice.astype(bf16), rows, preferred_element_type=f32).astype(bf16)


def exchange(rows):
    axes = ("far", "near", "tensor")
    return lax.all_to_all(rows, axes, split_axis=0, concat_axis=0, tiled=True)


def hold(*values):
    return lax.optimization_barrier(values)


def swap(rows, bit):
    size = lax.axis_size("tensor")
    return lax.ppermute(rows, "tensor", [(i, i ^ bit) for i in range(size)])


def gather_pieces(rows):
    far = swap(rows, 2)
    return rows, swap(rows, 1), far, swap(far, 1)


def to_slot(pieces, me):
    return place_rows(pieces, me ^ jnp.arange(4, dtype=jnp.int32))


def slot_piece(rows, me, other):
    size = rows.shape[0] // 4
    return lax.dynamic_slice_in_dim(rows, (me ^ other) * size, size)


def send_far(far_mate, far):
    return swap((far + swap(far_mate.astype(bf16), 1).astype(f32)).astype(bf16), 2)


def sum_group(came, mate, own):
    return own + swap(mate.astype(bf16), 1).astype(f32) + came.astype(f32)


def gather_weight(shard):
    return lax.all_gather(shard, ("far", "near"), axis=0, tiled=True)


def sum_weight(terms):
    return lax.psum_scatter(
        terms.astype(bf16), ("far", "near"), scatter_dimension=0, tiled=True
    ).astype(f32)


def to_near(rows):
    return lax.ppermute(rows, "near", [(0, 1), (1, 0)])


def to_far(rows, shift=1):
    size = lax.axis_size("far")
    return lax.ppermute(rows, "far", [(i, (i + shift) % size) for i in range(size)])


def gather_far(shard):
    return lax.all_gather(shard, "far", axis=0, tiled=False)


def far_direct(shard):
    return [to_far(shard, shift) if shift else shard for shift in range(lax.axis_size("far"))]


def both_near(mine, other, relative=False):
    size, near, far = lax.axis_size("far"), lax.axis_index("near"), lax.axis_index("far")
    spots = jnp.arange(size, dtype=jnp.int32)
    if relative:
        spots = lax.rem(far - spots + size, size)
    return place_rows(mine + other, jnp.concatenate([2 * spots + near, 2 * spots + 1 - near]))


def ring_step(held, last):
    return to_near(held), None if last else to_far(held)


def reduce_ring(parts):
    size, far, near = lax.axis_size("far"), lax.axis_index("far"), lax.axis_index("near")
    rows = parts[0].shape[0] // (2 * size)

    def share(place):
        return jnp.concatenate(
            [lax.dynamic_slice_in_dim(part, place * rows, rows) for part in parts], axis=1
        )

    held = None
    for step in range(size):
        place = lax.rem(far - 1 - step + 2 * size, size) * 2
        total = share(place + near).astype(f32) + to_near(share(place + 1 - near)).astype(f32)
        if held is not None:
            total = total + held.astype(f32)
        total = yield total
        if step < size - 1:
            held = to_far(total.astype(bf16))


def sum_far_first(terms):
    near = lax.axis_index("near")
    rows = lax.psum_scatter(terms.astype(bf16), "far", scatter_dimension=0, tiled=True)
    half = rows.shape[0] // 2
    take = lambda at: lax.dynamic_slice_in_dim(rows, at * half, half, axis=0)
    return take(near), take(1 - near)


def split_near(terms):
    size, near = lax.axis_size("far"), lax.axis_index("near")
    view = terms.astype(bf16).reshape(size, 2, -1, terms.shape[1])
    take = lambda at: lax.dynamic_slice_in_dim(view, at, 1, axis=1)[:, 0]
    return take(near), take(1 - near)


def add(mine, got):
    return (mine.astype(f32) + got.astype(f32)).astype(bf16)


def sum_far(terms):
    rows = terms.astype(bf16).reshape(-1, terms.shape[-1])
    return lax.psum_scatter(rows, "far", scatter_dimension=0, tiled=True).astype(f32)


def sum_all(part):
    part = part + to_near(part)
    for axis in ("tensor", "far"):
        size, bit = lax.axis_size(axis), 1
        while bit < size:
            part = part + lax.ppermute(part, axis, [(i, i ^ bit) for i in range(size)])
            bit *= 2
    return part


def dot(a, b, dims=NN):
    return lax.dot_general(a, b, dims, preferred_element_type=f32)


def shards(
    tokens, cotangent, w_in, w_beta, beta_bias, kernel, w_out, gain_attn, gain_ffn,
    w_gate, w_up, w_down, lengths, offsets, permutation, inverse,
):
    row_count = tokens.shape[0]
    me = lax.axis_index("tensor")
    group_rows = row_count * lax.axis_size("tensor")
    assert group_rows == SLOT and lax.axis_size("tensor") == 4
    heads = w_beta.shape[1]
    feats = w_in.shape[2]
    hidden_units = w_gate.shape[1]
    shard_rows = w_in.shape[0]
    at = jnp.arange(row_count, dtype=jnp.int32)

    send = rank_of(inverse)[None, :] == at[:, None]
    place = rank_of((permutation // row_count) * row_count + at)[:, None] == at[None, :]
    sent = pick_rows(send, tokens)
    narrow = jnp.pad(w_beta, ((0, 0), (0, HEADW - heads)))
    by_head = w_in.reshape(shard_rows, 4, heads, HEADW).transpose(0, 2, 1, 3)
    held = jnp.concatenate([by_head.reshape(shard_rows, 4 * feats), narrow], axis=1)
    size = lax.axis_size("far")
    cut = held.shape[1] // (2 * HEADW) * HEADW
    in_far = [gather_far(held[:, :cut]), gather_far(held[:, cut:])]
    dealt = pick_rows(place, exchange(sent)).astype(f32)

    positions = (
        (lax.axis_index("far") * 2 + lax.axis_index("near")) * group_rows
        + jnp.arange(group_rows, dtype=jnp.int32)
    )
    tables = attn_tables(seg_ids(positions, lengths, offsets), kernel.shape[0])
    bias_local = lax.dynamic_slice_in_dim(beta_bias, me * heads, heads)
    bias_row = jnp.pad(bias_local, (0, HEADW - heads))[None, :]
    taps = lax.dynamic_slice_in_dim(kernel, me * feats, feats, axis=1)

    normed = (dealt * rms_scale(dealt) * gain_attn[None, :]).astype(bf16)
    far = swap(normed, 2)
    in_far[0], w_gate, w_out = hold(in_far[0], w_gate, w_out.T)
    gate_far = gather_far(w_gate)
    in_twin = [to_near(in_far[0]), to_near(in_far[1])]
    in_far[1], w_up = hold(in_far[1], w_up)
    normed_all = to_slot((normed, swap(normed, 1), far, swap(far, 1)), me)
    spots = 2 * jnp.arange(size, dtype=jnp.int32)
    spots = jnp.concatenate([spots + lax.axis_index("near"), spots + 1 - lax.axis_index("near")] * 2)
    full_in = place_rows(
        [in_far[0], in_twin[0], in_far[1], in_twin[1]], spots, [0, 0, cut, cut], held.shape[1]
    )
    projected = dot(normed_all, full_in)
    out_far = far_direct(w_out)
    attended, *saved = attn_fwd(0, projected, bias_row, taps, *tables, ())
    attended, gate_far, w_up, *out_far = hold(attended, gate_far, w_up, *out_far)
    up_far = gather_far(w_up)
    gate_twin = to_near(gate_far)
    out_twin = to_near(jnp.concatenate(out_far))
    for head in range(1, heads):
        attended, *saved = attn_fwd(head, projected, bias_row, taps, *tables, [attended] + saved)
    attended, out_twin, gate_twin, up_far, w_down = hold(attended, out_twin, gate_twin, up_far, w_down.T)
    up_twin = to_near(up_far)
    down_far = gather_far(w_down)
    full_out = both_near(out_far, [out_twin.reshape((size,) + w_out.shape)], relative=True)

    att = [slot_piece(attended, me, other) for other in range(4)]
    term = lambda other: dot(att[other], full_out, NT)
    arrived_cot = exchange(pick_rows(send, cotangent))
    middle = dealt + sum_group(send_far(term(3), term(2)), term(1), term(0))
    normed2 = (middle * rms_scale(middle) * gain_ffn[None, :]).astype(bf16)
    far, mate = swap(normed2, 2), swap(normed2, 1)
    near_rows = jnp.concatenate([normed2, mate])
    full_gate = both_near([gate_far], [gate_twin])
    gate_near = dot(near_rows, full_gate)
    far, arrived_cot, up_twin, down_far, gate_near = hold(far, arrived_cot, up_twin, down_far, gate_near)
    down_twin = to_near(down_far)
    full_up = both_near([up_far], [up_twin])
    dealt_cot = pick_rows(place, arrived_cot)
    cot_near = jnp.concatenate([dealt_cot, swap(dealt_cot, 1)])
    cot_far = swap(dealt_cot, 2)
    far_rows = jnp.concatenate([far, swap(far, 1)])

    def forward(rows, gate_value):
        up_value = dot(rows, full_up)
        sig_gate = jax.nn.sigmoid(gate_value)
        return gate_value, up_value, sig_gate, (gate_value * sig_gate * up_value).astype(bf16)

    near_act, far_act = forward(near_rows, gate_near), forward(far_rows, dot(far_rows, full_gate))
    hidden_far, down_twin = hold(far_act[3], down_twin)
    full_down = both_near([down_far], [down_twin])
    cot_far = jnp.concatenate([cot_far, swap(cot_far, 1)])

    def backward(cot, act):
        gate_value, up_value, sig_gate, _ = act
        d_hidden = dot(cot, full_down)
        d_gate = d_hidden * up_value * sig_gate * (1.0 + gate_value * (1.0 - sig_gate))
        d_up = d_hidden * gate_value * sig_gate
        d_gate, d_up = d_gate.astype(bf16), d_up.astype(bf16)
        return d_gate, d_up, dot(d_gate, full_gate, NT) + dot(d_up, full_up, NT)

    d_gate_far, d_up_far, far_terms = backward(cot_far, far_act)
    came = send_far(far_terms[row_count:], far_terms[:row_count])
    d_gate_near, d_up_near, near_terms = backward(cot_near, near_act)
    join = lambda left, right: jnp.concatenate([left, right], axis=0)
    hidden, cot_rows, ffn_rows = join(near_act[3], hidden_far), join(cot_near, cot_far), join(near_rows, far_rows)
    d_wide = jnp.concatenate(
        [join(d_gate_near, d_gate_far), join(d_up_near, d_up_far)], axis=1
    )
    grad_wide = dot(ffn_rows, d_wide, TN).astype(bf16)
    ring = reduce_ring((grad_wide,))
    total = next(ring)
    grad_down = dot(cot_rows, hidden, TN).astype(bf16)
    came, grad_wide, grad_down = hold(came, grad_wide, grad_down)
    sum_down = sum_weight(grad_down)
    d_normed2 = sum_group(came, near_terms[row_count:], near_terms[:row_count])
    d_from_ffn, d_gain_ffn = rms_back(middle, gain_ffn, d_normed2)
    d_middle = dealt_cot.astype(f32) + d_from_ffn

    branch = d_middle.astype(bf16)
    far = swap(branch, 2)
    ffn_terms = dot(hidden, full_down, NT)
    far, ffn_terms = hold(far, ffn_terms)
    branch = (branch, swap(branch, 1), far, swap(far, 1))
    d_attended = to_slot([dot(piece, full_out) for piece in branch], me)
    grad_out = dot(jnp.concatenate(branch), jnp.concatenate(att), TN).astype(bf16)
    d_attended, ffn_terms, grad_out, total = hold(d_attended, ffn_terms, grad_out, total)
    total = ring.send(total)
    ffn_came = send_far(ffn_terms[3 * row_count :], ffn_terms[2 * row_count : 3 * row_count])
    d_projected, d_bias, d_taps = attn_bwd(projected, bias_row, taps, *tables, saved, d_attended)
    d_projected, ffn_came, total = hold(d_projected, ffn_came, total)
    total = ring.send(total)
    term_of = lambda other: dot(slot_piece(d_projected, me, other), full_in, NT)
    term = [None, None, term_of(2), term_of(3)]
    near_sum = term[2] + swap(term[3].astype(bf16), 1).astype(f32)
    near_sum, d_projected, middle, ffn_came = hold(near_sum.astype(bf16), d_projected, middle, ffn_came)
    came = swap(near_sum, 2)
    output = (middle + sum_group(ffn_came, ffn_terms[row_count : 2 * row_count], ffn_terms[:row_count])).astype(bf16)
    back = rank_of(permutation)[None, :] == at[:, None]
    home = rank_of((inverse // row_count) * row_count + at)[:, None] == at[None, :]
    grad_in = dot(normed_all, d_projected, TN).astype(bf16)
    grad_in, d_projected = hold(grad_in, d_projected)
    term[0], term[1] = term_of(0), term_of(1)
    d_gain_attn = (
        sum(jnp.sum(t * slot_piece(normed_all, me, o).astype(f32), axis=0) for o, t in enumerate(term))
        / gain_attn
    )
    sum_in = sum_weight(jnp.concatenate([grad_in, grad_out], axis=1))
    d_normed = sum_group(came, term[1], term[0])
    d_first, _ = rms_back(dealt, gain_attn, d_normed)
    d_input = (d_middle + d_first).astype(bf16)
    grad_sent, total = hold(pick_rows(back, d_input), total)
    grad_arrived = exchange(grad_sent)
    for step in range(3, size):
        total = ring.send(total)
    sum_wide = total
    grad_arrived, output = hold(grad_arrived, output)
    out_arrived = exchange(pick_rows(back, output))

    tap_terms = lax.dynamic_update_slice_in_dim(
        jnp.zeros(kernel.shape, f32), d_taps, me * feats, axis=1
    )
    bias_terms = lax.dynamic_update_slice_in_dim(
        jnp.zeros((1, kernel.shape[1]), f32), d_bias[:, :heads], me * heads, axis=1
    )
    small = sum_all(
        jnp.concatenate([tap_terms, bias_terms, d_gain_ffn[None, :], d_gain_attn[None, :]], axis=0)
    )
    tap_count = kernel.shape[0]
    sum_in, sum_out = sum_in[:, : grad_in.shape[1]], sum_in[:, grad_in.shape[1] :].T

    out_rows = pick_rows(home, out_arrived)
    grad_rows = pick_rows(home, grad_arrived)
    in_rows = sum_in[:, : 4 * feats].reshape(shard_rows, heads, 4, HEADW).transpose(0, 2, 1, 3)
    return (
        out_rows,
        grad_rows,
        in_rows.reshape(shard_rows, 4, feats),
        sum_in[:, 4 * feats : 4 * feats + heads],
        small[tap_count, : beta_bias.shape[0]],
        small[:tap_count],
        sum_out,
        small[tap_count + 2],
        small[tap_count + 1],
        sum_wide[:, :hidden_units],
        sum_wide[:, hidden_units:],
        sum_down.T,
    )


def solution(mesh):
    shape = mesh.devices.shape
    fine = Mesh(
        mesh.devices.reshape(shape[0] // 2, 2, shape[1]), ("far", "near", "tensor")
    )
    dp = ("far", "near")
    both, rows = P(("far", "near", "tensor")), P(("far", "near", "tensor"), None)
    in_specs = (
        rows, rows, P(dp, None, "tensor"), P(dp, "tensor"), P(), P(), P("tensor", dp), P(), P(),
        P(dp, "tensor"), P(dp, "tensor"), P("tensor", dp), P(), P(), both, both,
    )
    out_specs = (
        rows, rows, P(dp, None, "tensor"), P(dp, "tensor"), P(), P(), P("tensor", dp), P(), P(),
        P(dp, "tensor"), P(dp, "tensor"), P("tensor", dp),
    )
    return jax.shard_map(shards, mesh=fine, in_specs=in_specs, out_specs=out_specs, check_vma=False)
```

```python
import functools
import jax
import jax.numpy as jnp
from jax import lax
from jax.experimental import pallas as pl
from jax.experimental.pallas import tpu as pltpu
from jax.sharding import Mesh, PartitionSpec as P

SLOT = 1024
eps_norm = 1e-06

BLK = 128
HEADW = 128
eps_unit = 1e-06
f32, bf16 = jnp.float32, jnp.bfloat16
NN = (((1,), (0,)), ((), ()))
NT = (((1,), (1,)), ((), ()))
TN = (((0,), (0,)), ((), ()))


def bdims(dims):
    (a, b), _ = dims
    return ((tuple(i + 1 for i in a), tuple(i + 1 for i in b)), ((0,), (0,)))


def dot1(a, b, dims):
    return lax.dot_general(a, b, dims if a.ndim == 2 else bdims(dims), preferred_element_type=f32)


def split(x):
    hi = x.astype(bf16)
    return hi, (x - hi.astype(f32)).astype(bf16)


def dot3(a, b, dims):
    return dot1(a[0], b[0], dims) + (dot1(a[0], b[1], dims) + dot1(a[1], b[0], dims))


def iota2(rows, cols):
    r = lax.broadcasted_iota(jnp.int32, (rows, cols), 0)
    c = lax.broadcasted_iota(jnp.int32, (rows, cols), 1)
    return r, c


def convolve(w, taps, link):
    mixed = w * taps[0:1]
    for t in range(1, taps.shape[0]):
        mixed = mixed + (pltpu.roll(w, t, 0) * link[:, t : t + 1]) * taps[t : t + 1]
    return mixed


def unit_inverse(low, r, c):
    same8 = ((r // 8) == (c // 8))[None]
    n1 = jnp.where(same8, low, 0.0)
    s1 = split(n1)
    n2 = dot3(s1, s1, NN)
    s2 = split(n2)
    n4 = dot3(s2, s2, NN)
    x = jnp.where(r == c, 1.0, 0.0)[None] - n1
    x = x + dot3(split(x), s2, NN)
    x = x + dot3(split(x), split(n4), NN)
    size = 8
    while size < BLK:
        level = (((r // (2 * size)) == (c // (2 * size))) & ((r // size) != (c // size)))[None]
        part = jnp.where(level, low, 0.0)
        sx = split(x)
        x = x - dot3(split(dot3(sx, split(part), NN)), sx, NN)
        size *= 2
    return x


def pick_logit(tail_ref, bias_ref, head):
    lane = lax.broadcasted_iota(jnp.int32, (1, tail_ref.shape[1]), 1)
    return jnp.sum(jnp.where(lane == head, tail_ref[...] + bias_ref[...], 0.0), axis=1, keepdims=True)


def fwd_body(q_ref, k_ref, v_ref, w_ref, tail_ref, bias_ref, tap_ref, link_ref, segc_ref, segr_ref,
             o_ref, lse_ref, u_ref, gram_ref, tinv_ref, tr_ref, qt_ref, p_ref, sd_ref, hist_ref,
             kct, bl, *, group, head):
    length = q_ref.shape[0]
    blocks = length // BLK
    bl[...] = pick_logit(tail_ref, bias_ref, head)
    mixed = convolve(w_ref[...], tap_ref[...], link_ref[...])
    inv = lax.rsqrt(jnp.sum(mixed * mixed, axis=1, keepdims=True) + eps_unit)
    u_ref[0] = mixed * inv
    r, c = iota2(BLK, BLK)

    def phase1(g, _):
        rows = pl.ds(pl.multiple_of(g * group * BLK, BLK), group * BLK)
        three = lambda x: x.reshape(group, BLK, x.shape[-1])
        u = three(u_ref[0, rows, :])
        qb = three(q_ref[rows, :]).astype(bf16)
        kb = three(k_ref[rows, :]).astype(bf16)
        beta = three(2.0 * jax.nn.sigmoid(bl[rows, :]))
        sc = three(segc_ref[rows, :])
        sr = segr_ref[pl.ds(g * group, group)]
        same = sc == sr
        strict = same & (r > c)[None]
        upper = same & (r <= c)[None]
        u2 = split(u)
        uk = dot1(u2[0], kb, NT) + dot1(u2[1], kb, NT)
        uq = dot1(u2[0], qb, NT) + dot1(u2[1], qb, NT)
        s = jnp.where(strict, dot3(u2, u2, NT), 0.0)
        w = jnp.where(strict, uk, 0.0)
        rqt = jnp.where(upper, uq, 0.0)
        blk = pl.ds(g * group, group)
        gram_ref[0, blk, :, 0:BLK] = s
        gram_ref[0, blk, :, BLK : 2 * BLK] = rqt
        gram_ref[0, blk, :, 2 * BLK :] = w
        tinv = unit_inverse(beta * s, r, c)
        tinv_ref[0, blk] = tinv
        t2 = split(tinv)
        tr_u = dot3(t2, split(beta * u), NN)
        tr_w = dot3(t2, split(beta * w), NN)
        tr_ref[0, blk, :, 0:BLK] = tr_u
        tr_ref[0, blk, :, BLK:] = tr_w
        rq2 = split(rqt)
        tru2, trw2 = split(tr_u), split(tr_w)
        qt_ref[0, blk] = (qb.astype(f32) - dot3(rq2, tru2, TN)).astype(bf16)
        sd_ref[0, blk] = dot1(qb, kb, NT) - dot3(rq2, trw2, TN)
        p_ref[0, blk] = (jnp.where(r == c, 1.0, 0.0)[None] - dot3(u2, tru2, TN)).astype(bf16)
        kt = dot3(u2, trw2, TN)
        for i in range(group):
            kct[g * group + i] = (kb[i].astype(f32).T - kt[i]).astype(bf16)
        return 0

    lax.fori_loop(0, blocks // group, phase1, 0)
    scale = HEADW ** -0.5
    base = 0
    hist = None
    for b in range(blocks):
        n = b * BLK
        rows = pl.ds(n, BLK)
        same = segc_ref[rows, :] == segr_ref[b]
        diag = jnp.where(same & (r >= c), sd_ref[0, b] * scale, -1e30)
        top = jnp.max(diag, axis=1, keepdims=True)
        if b:
            off = dot1(qt_ref[0, b], hist_ref[0, :, pl.ds(base, n)], NN) * scale
            pieces = []
            for j in range(b):
                link = segc_ref[rows, :] == segr_ref[j]
                pieces.append(jnp.where(link, off[:, j * BLK : (j + 1) * BLK], -1e30))
            off = jnp.concatenate(pieces, axis=1)
            top = jnp.maximum(top, jnp.max(off, axis=1, keepdims=True))
            ed, eo = jnp.exp(diag - top), jnp.exp(off - top)
            total = jnp.sum(ed, axis=1, keepdims=True) + jnp.sum(eo, axis=1, keepdims=True)
            out = dot1(ed.astype(bf16), v_ref[rows, :].astype(bf16), NN) + dot1(
                eo.astype(bf16), v_ref[pl.ds(0, n), :].astype(bf16), NN)
        else:
            ed = jnp.exp(diag - top)
            total = jnp.sum(ed, axis=1, keepdims=True)
            out = dot1(ed.astype(bf16), v_ref[rows, :].astype(bf16), NN)
        o_ref[rows, :] = (out / total).astype(bf16)
        lse_ref[0, rows, :] = top + jnp.log(total)
        if b < blocks - 1:
            nxt = base + n
            if b:
                moved = dot1(p_ref[0, b], hist_ref[0, :, pl.ds(base, n)], NN)
                hist_ref[0, :, pl.ds(nxt, n)] = moved.astype(bf16)
            hist_ref[0, :, pl.ds(nxt + n, BLK)] = kct[b]
            base = nxt


def bwd_body(q_ref, k_ref, v_ref, w_ref, tail_ref, bias_ref, tap_ref, link_ref, segc_ref, segr_ref,
             lse_ref, u_ref, gram_ref, tinv_ref, tr_ref, qt_ref, p_ref, sd_ref, hist_ref, do_ref,
             dproj_ref, dbias_ref, dtap_ref,
             dkc, dvt, dz, du, bl, *, group, heads):
    head = pl.program_id(0)
    length = q_ref.shape[0]
    blocks = length // BLK
    scale = HEADW ** -0.5
    r, c = iota2(BLK, BLK)
    bl[...] = pick_logit(tail_ref, bias_ref, head)
    lane = lax.broadcasted_iota(jnp.int32, (1, HEADW), 1)

    @pl.when(head == 0)
    def _():
        dproj_ref[:, 4 * heads * HEADW :] = jnp.zeros((length, HEADW), bf16)
        dbias_ref[...] = jnp.zeros_like(dbias_ref)

    dkc[...] = jnp.zeros_like(dkc)
    dvt[...] = jnp.zeros_like(dvt)
    base = sum(range(blocks - 1)) * BLK
    for b in reversed(range(blocks)):
        n = b * BLK
        rows = pl.ds(n, BLK)
        lse = lse_ref[0, rows, :]
        same = segc_ref[rows, :] == segr_ref[b]
        pd = jnp.exp(jnp.where(same & (r >= c), sd_ref[0, b] * scale, -1e30) - lse)
        do = do_ref[rows, :]
        dob = do.astype(bf16)
        dot_t = do.T.astype(bf16)
        dpd = dot1(dob, v_ref[rows, :].astype(bf16), NT)
        delta = jnp.sum(pd * dpd, axis=1, keepdims=True)
        if b:
            kc = hist_ref[0, :, pl.ds(base, n)]
            off = dot1(qt_ref[0, b], kc, NN) * scale - lse
            pieces = []
            for j in range(b):
                link = segc_ref[rows, :] == segr_ref[j]
                pieces.append(jnp.where(link, off[:, j * BLK : (j + 1) * BLK], -1e30))
            po = jnp.exp(jnp.concatenate(pieces, axis=1))
            dpo = dot1(dob, v_ref[pl.ds(0, n), :].astype(bf16), NT)
            delta = delta + jnp.sum(po * dpo, axis=1, keepdims=True)
            go = (po * (dpo - delta) * scale).astype(bf16)
            dvt[:, pl.ds(0, n)] += dot1(dot_t, po.astype(bf16), NN)
        dvt[:, rows] += dot1(dot_t, pd.astype(bf16), NN)
        dz[b, 0:BLK, BLK:] = pd * (dpd - delta) * scale
        dz[b, BLK:, BLK:] = dkc[:, rows]
        if b:
            dz[b, 0:BLK, 0:BLK] = dot1(go, kc, NT)
            old = dkc[:, pl.ds(0, n)].astype(bf16)
            dz[b, BLK:, 0:BLK] = dot1(old, kc, NT)
            qtt = qt_ref[0, b].astype(f32).T.astype(bf16)
            dkc[:, pl.ds(0, n)] = dot1(p_ref[0, b], old, TN) + dot1(qtt, go, NN)
            base -= (b - 1) * BLK
        else:
            dz[b, 0:BLK, 0:BLK] = jnp.zeros((BLK, BLK), f32)
            dz[b, BLK:, 0:BLK] = jnp.zeros((BLK, BLK), f32)

    col = lambda part: pl.ds(pl.multiple_of((4 * head + part) * HEADW, HEADW), HEADW)

    def phase2(g, _):
        rows = pl.ds(pl.multiple_of(g * group * BLK, BLK), group * BLK)
        blk = pl.ds(g * group, group)
        three = lambda x: x.reshape(group, BLK, x.shape[-1])
        flat = lambda x: x.reshape(group * BLK, x.shape[-1])
        u = three(u_ref[0, rows, :])
        qb = three(q_ref[rows, :]).astype(bf16)
        kb = three(k_ref[rows, :]).astype(bf16)
        sig = three(jax.nn.sigmoid(bl[rows, :]))
        beta = 2.0 * sig
        same = three(segc_ref[rows, :]) == segr_ref[blk]
        strict = same & (r > c)[None]
        upper = same & (r <= c)[None]
        gram = gram_ref[0, blk]
        s, rqt, w = gram[:, :, :BLK], gram[:, :, BLK : 2 * BLK], gram[:, :, 2 * BLK :]
        t2 = split(tinv_ref[0, blk])
        tr = tr_ref[0, blk]
        tr2 = split(tr)
        z2 = split(dz[blk])
        left2 = split(jnp.concatenate([rqt, u], axis=2))
        lti2 = split(dot3(t2, left2, TN))
        yi = dot3(lti2, z2, NN)
        r2 = jnp.concatenate([u, w], axis=2) - dot1(s.astype(bf16), tr2[0], NN)
        dbeta = -jnp.sum(yi * r2, axis=2, keepdims=True)
        dlogit = jnp.where(lane == head, flat(dbeta * beta * (1.0 - sig)), 0.0)
        tail = pl.ds(4 * heads * HEADW, HEADW)
        dproj_ref[rows, tail] = jnp.where(lane == head, dlogit.astype(bf16), dproj_ref[rows, tail])
        dbias_ref[...] += jnp.sum(dlogit, axis=0, keepdims=True)
        y = beta * yi
        dlt = -dot3(tr2, z2, NT)
        ds = jnp.where(strict, dot3(split(y), tr2, NT), 0.0)
        drqt = jnp.where(upper, dlt[:, :, :BLK], 0.0)
        dw = jnp.where(strict, -y[:, :, BLK:], 0.0)
        ub = u.astype(bf16)
        drqb, dwb, dsb = drqt.astype(bf16), dw.astype(bf16), ds.astype(bf16)
        gd = dz[blk, 0:BLK, BLK:].astype(bf16)
        du[rows, :] = flat(
            dlt[:, :, BLK:] - y[:, :, :BLK] + dot1(drqb, qb, NN) + dot1(dwb, kb, NN)
            + dot1(dsb, ub, NN) + dot1(dsb, ub, TN))
        dq = dz[blk, 0:BLK, 0:BLK] + dot1(gd, kb, NN) + dot1(drqb, ub, TN)
        dproj_ref[rows, col(0)] = flat(dq).astype(bf16)
        dk = dot1(gd, qb, TN) + dot1(dwb, ub, TN)
        dkt = dz[blk, BLK:, BLK:]
        for i in range(group):
            here = pl.ds(pl.multiple_of((g * group + i) * BLK, BLK), BLK)
            dproj_ref[here, col(1)] = (dk[i] + dkt[i].T).astype(bf16)
            dproj_ref[here, col(2)] = dvt[:, here].T.astype(bf16)
        return 0

    lax.fori_loop(0, blocks // group, phase2, 0)
    taps, link, wv = tap_ref[...], link_ref[...], w_ref[...]
    mixed = convolve(wv, taps, link)
    inv = lax.rsqrt(jnp.sum(mixed * mixed, axis=1, keepdims=True) + eps_unit)
    duv = du[...]
    dm = inv * duv - mixed * ((inv * inv * inv) * jnp.sum(duv * mixed, axis=1, keepdims=True))
    dwr = dm * taps[0:1]
    dtap_ref[0:1, :] = jnp.sum(dm * wv, axis=0, keepdims=True)
    for t in range(1, taps.shape[0]):
        dml = dm * link[:, t : t + 1]
        dwr = dwr + pltpu.roll(dml, length - t, 0) * taps[t : t + 1]
        dtap_ref[t : t + 1, :] = jnp.sum(dml * pltpu.roll(wv, t, 0), axis=0, keepdims=True)
    dproj_ref[:, col(3)] = dwr.astype(bf16)


def attn_specs(length, heads, head_of, ntap):
    blocks = length // BLK
    part = lambda p: pl.BlockSpec((length, HEADW), lambda i: (0, 4 * head_of(i) + p))
    ins = [part(0), part(1), part(2), part(3),
           pl.BlockSpec((length, HEADW), lambda i: (0, 4 * heads)),
           pl.BlockSpec((1, HEADW), lambda i: (0, 0)),
           pl.BlockSpec((ntap, HEADW), lambda i: (0, head_of(i))),
           pl.BlockSpec((length, ntap), lambda i: (0, 0)),
           pl.BlockSpec((length, 1), lambda i: (0, 0)),
           pl.BlockSpec((blocks, 1, BLK), lambda i: (0, 0, 0))]
    tri = blocks * (blocks - 1) // 2 * BLK
    shapes = [((length, 1), f32), ((length, HEADW), f32), ((blocks, BLK, 3 * BLK), f32),
              ((blocks, BLK, BLK), f32), ((blocks, BLK, 2 * BLK), f32), ((blocks, BLK, BLK), bf16),
              ((blocks, BLK, BLK), bf16), ((blocks, BLK, BLK), f32), ((BLK, tri), bf16)]
    saved = [jax.ShapeDtypeStruct((heads,) + s, d) for s, d in shapes]
    saved_specs = [
        pl.BlockSpec((1,) + s, (lambda i: (head_of(i), 0, 0)) if len(s) == 2 else (lambda i: (head_of(i), 0, 0, 0)))
        for s, _ in shapes
    ]
    return ins, saved, saved_specs


def attn_fwd(head, proj, bias, taps, link, segc, segr, before, group=4):
    length, heads = proj.shape[0], taps.shape[1] // HEADW
    ins, saved, saved_specs = attn_specs(length, heads, lambda i: head, taps.shape[0])
    out_specs = [pl.BlockSpec((length, HEADW), lambda i: (0, head))] + saved_specs
    out_shape = [jax.ShapeDtypeStruct((length, heads * HEADW), bf16)] + saved
    count = len(ins)

    def body(*refs):
        fwd_body(*refs[:count], *refs[count + len(before) :], group=group, head=head)

    return pl.pallas_call(
        body,
        grid=(1,),
        in_specs=ins + [pl.BlockSpec(memory_space=pl.ANY)] * len(before),
        out_specs=out_specs,
        out_shape=out_shape,
        input_output_aliases={count + i: i for i in range(len(before))},
        scratch_shapes=[pltpu.VMEM((length // BLK, BLK, BLK), bf16), pltpu.VMEM((length, 1), f32)],
        compiler_params=pltpu.CompilerParams(vmem_limit_bytes=58 << 20),
        cost_estimate=pl.CostEstimate(flops=4 * 10**9, bytes_accessed=1 << 20, transcendentals=10**6),
        name="path_fwd",
    )(proj, proj, proj, proj, proj, bias, taps, link, segc, segr, *before)


def attn_bwd(proj, bias, taps, link, segc, segr, saved, d_att, group=4):
    length, heads = proj.shape[0], taps.shape[1] // HEADW
    ins, _, saved_specs = attn_specs(length, heads, lambda i: i, taps.shape[0])
    blocks = length // BLK
    width = (4 * heads + 1) * HEADW
    return pl.pallas_call(
        functools.partial(bwd_body, group=group, heads=heads),
        grid=(heads,),
        in_specs=ins + saved_specs + [pl.BlockSpec((length, HEADW), lambda i: (0, i))],
        out_specs=[pl.BlockSpec((length, width), lambda i: (0, 0)),
                   pl.BlockSpec((1, HEADW), lambda i: (0, 0)),
                   pl.BlockSpec((taps.shape[0], HEADW), lambda i: (0, i))],
        out_shape=[jax.ShapeDtypeStruct((length, width), bf16),
                   jax.ShapeDtypeStruct((1, HEADW), f32),
                   jax.ShapeDtypeStruct(taps.shape, f32)],
        scratch_shapes=[pltpu.VMEM((BLK, length), f32), pltpu.VMEM((BLK, length), f32),
                        pltpu.VMEM((blocks, 2 * BLK, 2 * BLK), f32), pltpu.VMEM((length, HEADW), f32),
                        pltpu.VMEM((length, 1), f32)],
        compiler_params=pltpu.CompilerParams(vmem_limit_bytes=60 << 20),
        cost_estimate=pl.CostEstimate(flops=10**9, bytes_accessed=1 << 20, transcendentals=10**6),
        name="path_bwd",
    )(proj, proj, proj, proj, proj, bias, taps, link, segc, segr, *saved, d_att)


def place_body(shapes, columns, rows, at_ref, *refs):
    out, count = refs[len(shapes)], 0
    for source, shape, column in zip(refs, shapes, columns):
        for piece in [source] if len(shape) == 2 else [source.at[i] for i in range(shape[0])]:
            first = pl.multiple_of(at_ref[count] * rows, rows)
            out[pl.ds(first, rows), pl.ds(column, shape[-1])] = piece[...]
            count += 1


def place_rows(sources, places, columns=None, width=None):
    columns = columns or [0] * len(sources)
    width = width or sources[0].shape[-1]
    rows, kind = sources[0].shape[-2], sources[0].dtype
    total = sum(source.size for source in sources)
    size = 2 * total * kind.itemsize
    whole = lambda shape: pl.BlockSpec(shape, lambda i, at: (0,) * len(shape))
    return pl.pallas_call(
        functools.partial(place_body, [source.shape for source in sources], columns, rows),
        grid_spec=pltpu.PrefetchScalarGridSpec(
            num_scalar_prefetch=1,
            grid=(1,),
            in_specs=[whole(source.shape) for source in sources],
            out_specs=whole((total // width, width)),
        ),
        out_shape=jax.ShapeDtypeStruct((total // width, width), kind),
        compiler_params=pltpu.CompilerParams(vmem_limit_bytes=(2 * size) + (4 << 20)),
        cost_estimate=pl.CostEstimate(flops=0, bytes_accessed=size, transcendentals=0),
        name="place_rows",
    )(places, *sources)


def attn_tables(segment, ntap):
    length = segment.shape[0]
    at = jnp.arange(length, dtype=jnp.int32)
    ids = jnp.where(segment >= 0, segment, -1 - at)
    link = [jnp.ones((length,), f32)]
    for t in range(1, ntap):
        same = jnp.concatenate([jnp.zeros((t,), bool), ids[t:] == ids[:-t]])
        link.append(same.astype(f32))
    return jnp.stack(link, axis=1), ids[:, None], ids.reshape(length // BLK, 1, BLK)


def seg_ids(positions, lengths, offsets):
    inside = (positions[:, None] >= offsets[None, :]) & (
        positions[:, None] < offsets[None, :] + lengths[None, :]
    )
    number = jnp.arange(1, offsets.shape[0] + 1, dtype=jnp.int32)
    return jnp.sum(jnp.where(inside, number[None, :], 0), axis=1) - 1


def rms_scale(values):
    return lax.rsqrt(jnp.mean(values * values, axis=1, keepdims=True) + eps_norm)


def rms_back(values, gain_vec, d_normed):
    inv_rms = rms_scale(values)
    scaled = d_normed * gain_vec[None, :]
    d_values = inv_rms * scaled - values * (inv_rms * inv_rms * inv_rms) * jnp.mean(
        scaled * values, axis=1, keepdims=True
    )
    d_gain = jnp.sum(d_normed * values * inv_rms, axis=0)
    return (d_values, d_gain)


def rank_of(keys):
    return jnp.sum((keys[None, :] < keys[:, None]).astype(jnp.int32), axis=1)


def pick_rows(choice, rows):
    return jnp.dot(choice.astype(bf16), rows, preferred_element_type=f32).astype(bf16)


def exchange(rows):
    axes = ("far", "near", "tensor")
    return lax.all_to_all(rows, axes, split_axis=0, concat_axis=0, tiled=True)


def hold(*values):
    return lax.optimization_barrier(values)


def swap(rows, bit):
    size = lax.axis_size("tensor")
    return lax.ppermute(rows, "tensor", [(i, i ^ bit) for i in range(size)])


def gather_pieces(rows):
    far = swap(rows, 2)
    return rows, swap(rows, 1), far, swap(far, 1)


def to_slot(pieces, me):
    return place_rows(pieces, me ^ jnp.arange(4, dtype=jnp.int32))


def slot_piece(rows, me, other):
    size = rows.shape[0] // 4
    return lax.dynamic_slice_in_dim(rows, (me ^ other) * size, size)


def send_far(far_mate, far):
    return swap((far + swap(far_mate.astype(bf16), 1).astype(f32)).astype(bf16), 2)


def sum_group(came, mate, own):
    return own + swap(mate.astype(bf16), 1).astype(f32) + came.astype(f32)


def gather_weight(shard):
    return lax.all_gather(shard, ("far", "near"), axis=0, tiled=True)


def sum_weight(terms):
    return lax.psum_scatter(
        terms.astype(bf16), ("far", "near"), scatter_dimension=0, tiled=True
    ).astype(f32)


def to_near(rows):
    return lax.ppermute(rows, "near", [(0, 1), (1, 0)])


def to_far(rows, shift=1):
    size = lax.axis_size("far")
    return lax.ppermute(rows, "far", [(i, (i + shift) % size) for i in range(size)])


def gather_far(shard):
    return lax.all_gather(shard, "far", axis=0, tiled=False)


def far_direct(shard):
    return [to_far(shard, shift) if shift else shard for shift in range(lax.axis_size("far"))]


def both_near(mine, other, relative=False):
    size, near, far = lax.axis_size("far"), lax.axis_index("near"), lax.axis_index("far")
    spots = jnp.arange(size, dtype=jnp.int32)
    if relative:
        spots = lax.rem(far - spots + size, size)
    return place_rows(mine + other, jnp.concatenate([2 * spots + near, 2 * spots + 1 - near]))


def ring_step(held, last):
    return to_near(held), None if last else to_far(held)


def reduce_ring(parts):
    size, far, near = lax.axis_size("far"), lax.axis_index("far"), lax.axis_index("near")
    rows = parts[0].shape[0] // (2 * size)

    def share(place):
        return jnp.concatenate(
            [lax.dynamic_slice_in_dim(part, place * rows, rows) for part in parts], axis=1
        )

    held = None
    for step in range(size):
        place = lax.rem(far - 1 - step + 2 * size, size) * 2
        total = share(place + near).astype(f32) + to_near(share(place + 1 - near)).astype(f32)
        if held is not None:
            total = total + held.astype(f32)
        total = yield total
        if step < size - 1:
            held = to_far(total.astype(bf16))


def sum_far_first(terms):
    near = lax.axis_index("near")
    rows = lax.psum_scatter(terms.astype(bf16), "far", scatter_dimension=0, tiled=True)
    half = rows.shape[0] // 2
    take = lambda at: lax.dynamic_slice_in_dim(rows, at * half, half, axis=0)
    return take(near), take(1 - near)


def split_near(terms):
    size, near = lax.axis_size("far"), lax.axis_index("near")
    view = terms.astype(bf16).reshape(size, 2, -1, terms.shape[1])
    take = lambda at: lax.dynamic_slice_in_dim(view, at, 1, axis=1)[:, 0]
    return take(near), take(1 - near)


def add(mine, got):
    return (mine.astype(f32) + got.astype(f32)).astype(bf16)


def sum_far(terms):
    rows = terms.astype(bf16).reshape(-1, terms.shape[-1])
    return lax.psum_scatter(rows, "far", scatter_dimension=0, tiled=True).astype(f32)


def sum_all(part):
    part = part + to_near(part)
    for axis in ("tensor", "far"):
        size, bit = lax.axis_size(axis), 1
        while bit < size:
            part = part + lax.ppermute(part, axis, [(i, i ^ bit) for i in range(size)])
            bit *= 2
    return part


def dot(a, b, dims=NN):
    return lax.dot_general(a, b, dims, preferred_element_type=f32)


def shards(
    tokens, cotangent, w_in, w_beta, beta_bias, kernel, w_out, gain_attn, gain_ffn,
    w_gate, w_up, w_down, lengths, offsets, permutation, inverse,
):
    row_count = tokens.shape[0]
    me = lax.axis_index("tensor")
    group_rows = row_count * lax.axis_size("tensor")
    assert group_rows == SLOT and lax.axis_size("tensor") == 4
    heads = w_beta.shape[1]
    feats = w_in.shape[2]
    hidden_units = w_gate.shape[1]
    shard_rows = w_in.shape[0]
    at = jnp.arange(row_count, dtype=jnp.int32)

    send = rank_of(inverse)[None, :] == at[:, None]
    place = rank_of((permutation // row_count) * row_count + at)[:, None] == at[None, :]
    sent = pick_rows(send, tokens)
    narrow = jnp.pad(w_beta, ((0, 0), (0, HEADW - heads)))
    by_head = w_in.reshape(shard_rows, 4, heads, HEADW).transpose(0, 2, 1, 3)
    held = jnp.concatenate([by_head.reshape(shard_rows, 4 * feats), narrow], axis=1)
    size = lax.axis_size("far")
    cut, width = held.shape[1] // (2 * HEADW) * HEADW, held.shape[1]
    in_first = gather_weight(held[:, :cut])
    held = held[:, cut:]
    pieces = []

    def hop(held, last=False):
        twin, later = ring_step(held, last)
        pieces.append((held, twin))
        return later

    arrived = exchange(sent)
    for _ in range(size // 2):
        held = hop(held)
    arrived, held = hold(arrived, held)
    for _ in range(size // 2, size - 1):
        held = hop(held)
    hop(held, True)
    dealt = pick_rows(place, arrived).astype(f32)

    positions = (
        (lax.axis_index("far") * 2 + lax.axis_index("near")) * group_rows
        + jnp.arange(group_rows, dtype=jnp.int32)
    )
    tables = attn_tables(seg_ids(positions, lengths, offsets), kernel.shape[0])
    bias_local = lax.dynamic_slice_in_dim(beta_bias, me * heads, heads)
    bias_row = jnp.pad(bias_local, (0, HEADW - heads))[None, :]
    taps = lax.dynamic_slice_in_dim(kernel, me * feats, feats, axis=1)

    normed = (dealt * rms_scale(dealt) * gain_attn[None, :]).astype(bf16)
    far = swap(normed, 2)
    in_first, w_gate, w_out = hold(in_first, w_gate, w_out.T)
    gate_far = gather_far(w_gate)
    normed_all = to_slot((normed, swap(normed, 1), far, swap(far, 1)), me)
    spots = jnp.arange(size, dtype=jnp.int32)
    spots, near = 2 * lax.rem(lax.axis_index("far") - spots + size, size), lax.axis_index("near")
    full_in = place_rows(
        [in_first.reshape(2 * size, shard_rows, cut)] + [p[0] for p in pieces] + [p[1] for p in pieces],
        jnp.concatenate([jnp.arange(2 * size, dtype=jnp.int32), spots + near, spots + 1 - near]),
        [0] + [cut] * (2 * size), width,
    )
    projected = dot(normed_all, full_in)
    out_far = far_direct(w_out)
    attended, *saved = attn_fwd(0, projected, bias_row, taps, *tables, ())
    attended, *out_far = hold(attended, *out_far)
    out_twin = to_near(jnp.concatenate(out_far))
    attended, *saved = attn_fwd(1, projected, bias_row, taps, *tables, [attended] + saved)
    attended, gate_far, w_up = hold(attended, gate_far, w_up)
    gate_twin = to_near(gate_far)
    up_far = gather_far(w_up)
    for head in range(2, heads):
        attended, *saved = attn_fwd(head, projected, bias_row, taps, *tables, [attended] + saved)
    attended, out_twin, w_down = hold(attended, out_twin, w_down.T)
    down_far = gather_far(w_down)
    full_out = both_near(out_far, [out_twin.reshape((size,) + w_out.shape)], relative=True)

    att = [slot_piece(attended, me, other) for other in range(4)]
    term = lambda other: dot(att[other], full_out, NT)
    arrived_cot = exchange(pick_rows(send, cotangent))
    came, up_far, gate_twin = hold(send_far(term(3), term(2)), up_far, gate_twin)
    up_twin = to_near(up_far)
    middle = dealt + sum_group(came, term(1), term(0))
    normed2 = (middle * rms_scale(middle) * gain_ffn[None, :]).astype(bf16)
    far, mate = swap(normed2, 2), swap(normed2, 1)
    near_rows = jnp.concatenate([normed2, mate])
    full_gate = both_near([gate_far], [gate_twin])
    gate_near = dot(near_rows, full_gate)
    far, arrived_cot, up_twin, down_far, gate_near = hold(far, arrived_cot, up_twin, down_far, gate_near)
    down_twin = to_near(down_far)
    full_up = both_near([up_far], [up_twin])
    dealt_cot = pick_rows(place, arrived_cot)
    cot_near = jnp.concatenate([dealt_cot, swap(dealt_cot, 1)])
    cot_far = swap(dealt_cot, 2)
    far_rows = jnp.concatenate([far, swap(far, 1)])

    def forward(rows, gate_value):
        up_value = dot(rows, full_up)
        sig_gate = jax.nn.sigmoid(gate_value)
        return gate_value, up_value, sig_gate, (gate_value * sig_gate * up_value).astype(bf16)

    near_act, far_act = forward(near_rows, gate_near), forward(far_rows, dot(far_rows, full_gate))
    hidden_far, down_twin = hold(far_act[3], down_twin)
    full_down = both_near([down_far], [down_twin])
    cot_far = jnp.concatenate([cot_far, swap(cot_far, 1)])

    def backward(cot, act):
        gate_value, up_value, sig_gate, _ = act
        d_hidden = dot(cot, full_down)
        d_gate = d_hidden * up_value * sig_gate * (1.0 + gate_value * (1.0 - sig_gate))
        d_up = d_hidden * gate_value * sig_gate
        d_gate, d_up = d_gate.astype(bf16), d_up.astype(bf16)
        return d_gate, d_up, dot(d_gate, full_gate, NT) + dot(d_up, full_up, NT)

    d_gate_far, d_up_far, far_terms = backward(cot_far, far_act)
    far_sum = far_terms[:row_count] + swap(far_terms[row_count:].astype(bf16), 1).astype(f32)
    far_sum, cot_near, d_gate_far = hold(far_sum.astype(bf16), cot_near, d_gate_far)
    came = swap(far_sum, 2)
    d_gate_near, d_up_near, near_terms = backward(cot_near, near_act)
    join = lambda left, right: jnp.concatenate([left, right], axis=0)
    hidden, cot_rows, ffn_rows = join(near_act[3], hidden_far), join(cot_near, cot_far), join(near_rows, far_rows)
    d_wide = jnp.concatenate(
        [join(d_gate_near, d_gate_far), join(d_up_near, d_up_far)], axis=1
    )
    grad_wide = dot(ffn_rows, d_wide, TN).astype(bf16)
    ring = reduce_ring((grad_wide,))
    total = next(ring)
    grad_down = dot(cot_rows, hidden, TN).astype(bf16)
    came, grad_wide, grad_down = hold(came, grad_wide, grad_down)
    sum_down = sum_weight(grad_down)
    d_normed2 = sum_group(came, near_terms[row_count:], near_terms[:row_count])
    d_from_ffn, d_gain_ffn = rms_back(middle, gain_ffn, d_normed2)
    d_middle = dealt_cot.astype(f32) + d_from_ffn

    branch = d_middle.astype(bf16)
    far = swap(branch, 2)
    ffn_terms = dot(hidden, full_down, NT)
    far, ffn_terms = hold(far, ffn_terms)
    branch = (branch, swap(branch, 1), far, swap(far, 1))
    d_attended = to_slot([dot(piece, full_out) for piece in branch], me)
    grad_out = dot(jnp.concatenate(branch), jnp.concatenate(att), TN).astype(bf16)
    d_attended, ffn_terms, grad_out, total = hold(d_attended, ffn_terms, grad_out, total)
    total = ring.send(total)
    ffn_came = send_far(ffn_terms[3 * row_count :], ffn_terms[2 * row_count : 3 * row_count])
    d_projected, d_bias, d_taps = attn_bwd(projected, bias_row, taps, *tables, saved, d_attended)
    d_projected, ffn_came, total = hold(d_projected, ffn_came, total)
    total = ring.send(total)
    term_of = lambda other: dot(slot_piece(d_projected, me, other), full_in, NT)
    term = [None, None, term_of(2), term_of(3)]
    near_sum = term[2] + swap(term[3].astype(bf16), 1).astype(f32)
    near_sum, d_projected, middle, ffn_came = hold(near_sum.astype(bf16), d_projected, middle, ffn_came)
    came = swap(near_sum, 2)
    output = (middle + sum_group(ffn_came, ffn_terms[row_count : 2 * row_count], ffn_terms[:row_count])).astype(bf16)
    back = rank_of(permutation)[None, :] == at[:, None]
    home = rank_of((inverse // row_count) * row_count + at)[:, None] == at[None, :]
    grad_in = dot(normed_all, d_projected, TN).astype(bf16)
    grad_in, d_projected = hold(grad_in, d_projected)
    term[0], term[1] = term_of(0), term_of(1)
    d_gain_attn = (
        sum(jnp.sum(t * slot_piece(normed_all, me, o).astype(f32), axis=0) for o, t in enumerate(term))
        / gain_attn
    )
    part = grad_in.shape[1] // (2 * HEADW) * HEADW
    sum_in = sum_weight(jnp.concatenate([grad_in[:, :part], grad_out], axis=1))
    ring_in = reduce_ring((grad_in[:, part:],))
    total_in = next(ring_in)
    d_normed = sum_group(came, term[1], term[0])
    d_first, _ = rms_back(dealt, gain_attn, d_normed)
    d_input = (d_middle + d_first).astype(bf16)
    grad_sent, total, total_in = hold(pick_rows(back, d_input), total, total_in)
    grad_arrived = exchange(grad_sent)
    for step in range(3, size):
        total = ring.send(total)
    total_in = ring_in.send(total_in)
    sum_wide, total_in = hold(total, total_in)
    for step in range(2, size - 1):
        total_in = ring_in.send(total_in)
    grad_arrived, output, total_in = hold(grad_arrived, output, total_in)
    total_in = ring_in.send(total_in)
    out_arrived = exchange(pick_rows(back, output))

    tap_terms = lax.dynamic_update_slice_in_dim(
        jnp.zeros(kernel.shape, f32), d_taps, me * feats, axis=1
    )
    bias_terms = lax.dynamic_update_slice_in_dim(
        jnp.zeros((1, kernel.shape[1]), f32), d_bias[:, :heads], me * heads, axis=1
    )
    small = sum_all(
        jnp.concatenate([tap_terms, bias_terms, d_gain_ffn[None, :], d_gain_attn[None, :]], axis=0)
    )
    tap_count = kernel.shape[0]
    sum_in, sum_out = jnp.concatenate([sum_in[:, :part], total_in], axis=1), sum_in[:, part:].T

    out_rows = pick_rows(home, out_arrived)
    grad_rows = pick_rows(home, grad_arrived)
    in_rows = sum_in[:, : 4 * feats].reshape(shard_rows, heads, 4, HEADW).transpose(0, 2, 1, 3)
    return (
        out_rows,
        grad_rows,
        in_rows.reshape(shard_rows, 4, feats),
        sum_in[:, 4 * feats : 4 * feats + heads],
        small[tap_count, : beta_bias.shape[0]],
        small[:tap_count],
        sum_out,
        small[tap_count + 2],
        small[tap_count + 1],
        sum_wide[:, :hidden_units],
        sum_wide[:, hidden_units:],
        sum_down.T,
    )


def solution(mesh):
    shape = mesh.devices.shape
    fine = Mesh(
        mesh.devices.reshape(shape[0] // 2, 2, shape[1]), ("far", "near", "tensor")
    )
    dp = ("far", "near")
    both, rows = P(("far", "near", "tensor")), P(("far", "near", "tensor"), None)
    in_specs = (
        rows, rows, P(dp, None, "tensor"), P(dp, "tensor"), P(), P(), P("tensor", dp), P(), P(),
        P(dp, "tensor"), P(dp, "tensor"), P("tensor", dp), P(), P(), both, both,
    )
    out_specs = (
        rows, rows, P(dp, None, "tensor"), P(dp, "tensor"), P(), P(), P("tensor", dp), P(), P(),
        P(dp, "tensor"), P(dp, "tensor"), P("tensor", dp),
    )
    return jax.shard_map(shards, mesh=fine, in_specs=in_specs, out_specs=out_specs, check_vma=False)
```

```python
import functools
import jax
import jax.numpy as jnp
from jax import lax
from jax.experimental import pallas as pl
from jax.experimental.pallas import tpu as pltpu
from jax.sharding import Mesh, PartitionSpec as P

SLOT = 1024
eps_norm = 1e-06

BLK = 128
HEADW = 128
eps_unit = 1e-06
f32, bf16 = jnp.float32, jnp.bfloat16
NN = (((1,), (0,)), ((), ()))
NT = (((1,), (1,)), ((), ()))
TN = (((0,), (0,)), ((), ()))


def bdims(dims):
    (a, b), _ = dims
    return ((tuple(i + 1 for i in a), tuple(i + 1 for i in b)), ((0,), (0,)))


def dot1(a, b, dims):
    return lax.dot_general(a, b, dims if a.ndim == 2 else bdims(dims), preferred_element_type=f32)


def split(x):
    hi = x.astype(bf16)
    return hi, (x - hi.astype(f32)).astype(bf16)


def dot3(a, b, dims):
    return dot1(a[0], b[0], dims) + (dot1(a[0], b[1], dims) + dot1(a[1], b[0], dims))


def iota2(rows, cols):
    r = lax.broadcasted_iota(jnp.int32, (rows, cols), 0)
    c = lax.broadcasted_iota(jnp.int32, (rows, cols), 1)
    return r, c


def convolve(w, taps, link):
    mixed = w * taps[0:1]
    for t in range(1, taps.shape[0]):
        mixed = mixed + (pltpu.roll(w, t, 0) * link[:, t : t + 1]) * taps[t : t + 1]
    return mixed


def unit_inverse(low, r, c):
    same8 = ((r // 8) == (c // 8))[None]
    n1 = jnp.where(same8, low, 0.0)
    s1 = split(n1)
    n2 = dot3(s1, s1, NN)
    s2 = split(n2)
    n4 = dot3(s2, s2, NN)
    x = jnp.where(r == c, 1.0, 0.0)[None] - n1
    x = x + dot3(split(x), s2, NN)
    x = x + dot3(split(x), split(n4), NN)
    size = 8
    while size < BLK:
        level = (((r // (2 * size)) == (c // (2 * size))) & ((r // size) != (c // size)))[None]
        part = jnp.where(level, low, 0.0)
        sx = split(x)
        x = x - dot3(split(dot3(sx, split(part), NN)), sx, NN)
        size *= 2
    return x


def pick_logit(tail_ref, bias_ref, head):
    lane = lax.broadcasted_iota(jnp.int32, (1, tail_ref.shape[1]), 1)
    return jnp.sum(jnp.where(lane == head, tail_ref[...] + bias_ref[...], 0.0), axis=1, keepdims=True)


def fwd_body(q_ref, k_ref, v_ref, w_ref, tail_ref, bias_ref, tap_ref, link_ref, segc_ref, segr_ref,
             o_ref, lse_ref, u_ref, gram_ref, tinv_ref, tr_ref, qt_ref, p_ref, sd_ref, hist_ref,
             kct, bl, *, group, head):
    length = q_ref.shape[0]
    blocks = length // BLK
    bl[...] = pick_logit(tail_ref, bias_ref, head)
    mixed = convolve(w_ref[...], tap_ref[...], link_ref[...])
    inv = lax.rsqrt(jnp.sum(mixed * mixed, axis=1, keepdims=True) + eps_unit)
    u_ref[0] = mixed * inv
    r, c = iota2(BLK, BLK)

    def phase1(g, _):
        rows = pl.ds(pl.multiple_of(g * group * BLK, BLK), group * BLK)
        three = lambda x: x.reshape(group, BLK, x.shape[-1])
        u = three(u_ref[0, rows, :])
        qb = three(q_ref[rows, :]).astype(bf16)
        kb = three(k_ref[rows, :]).astype(bf16)
        beta = three(2.0 * jax.nn.sigmoid(bl[rows, :]))
        sc = three(segc_ref[rows, :])
        sr = segr_ref[pl.ds(g * group, group)]
        same = sc == sr
        strict = same & (r > c)[None]
        upper = same & (r <= c)[None]
        u2 = split(u)
        uk = dot1(u2[0], kb, NT) + dot1(u2[1], kb, NT)
        uq = dot1(u2[0], qb, NT) + dot1(u2[1], qb, NT)
        s = jnp.where(strict, dot3(u2, u2, NT), 0.0)
        w = jnp.where(strict, uk, 0.0)
        rqt = jnp.where(upper, uq, 0.0)
        blk = pl.ds(g * group, group)
        gram_ref[0, blk, :, 0:BLK] = s
        gram_ref[0, blk, :, BLK : 2 * BLK] = rqt
        gram_ref[0, blk, :, 2 * BLK :] = w
        tinv = unit_inverse(beta * s, r, c)
        tinv_ref[0, blk] = tinv
        t2 = split(tinv)
        tr_u = dot3(t2, split(beta * u), NN)
        tr_w = dot3(t2, split(beta * w), NN)
        tr_ref[0, blk, :, 0:BLK] = tr_u
        tr_ref[0, blk, :, BLK:] = tr_w
        rq2 = split(rqt)
        tru2, trw2 = split(tr_u), split(tr_w)
        qt_ref[0, blk] = (qb.astype(f32) - dot3(rq2, tru2, TN)).astype(bf16)
        sd_ref[0, blk] = dot1(qb, kb, NT) - dot3(rq2, trw2, TN)
        p_ref[0, blk] = (jnp.where(r == c, 1.0, 0.0)[None] - dot3(u2, tru2, TN)).astype(bf16)
        kt = dot3(u2, trw2, TN)
        for i in range(group):
            kct[g * group + i] = (kb[i].astype(f32).T - kt[i]).astype(bf16)
        return 0

    lax.fori_loop(0, blocks // group, phase1, 0)
    scale = HEADW ** -0.5
    base = 0
    hist = None
    for b in range(blocks):
        n = b * BLK
        rows = pl.ds(n, BLK)
        same = segc_ref[rows, :] == segr_ref[b]
        diag = jnp.where(same & (r >= c), sd_ref[0, b] * scale, -1e30)
        top = jnp.max(diag, axis=1, keepdims=True)
        if b:
            off = dot1(qt_ref[0, b], hist_ref[0, :, pl.ds(base, n)], NN) * scale
            pieces = []
            for j in range(b):
                link = segc_ref[rows, :] == segr_ref[j]
                pieces.append(jnp.where(link, off[:, j * BLK : (j + 1) * BLK], -1e30))
            off = jnp.concatenate(pieces, axis=1)
            top = jnp.maximum(top, jnp.max(off, axis=1, keepdims=True))
            ed, eo = jnp.exp(diag - top), jnp.exp(off - top)
            total = jnp.sum(ed, axis=1, keepdims=True) + jnp.sum(eo, axis=1, keepdims=True)
            out = dot1(ed.astype(bf16), v_ref[rows, :].astype(bf16), NN) + dot1(
                eo.astype(bf16), v_ref[pl.ds(0, n), :].astype(bf16), NN)
        else:
            ed = jnp.exp(diag - top)
            total = jnp.sum(ed, axis=1, keepdims=True)
            out = dot1(ed.astype(bf16), v_ref[rows, :].astype(bf16), NN)
        o_ref[rows, :] = (out / total).astype(bf16)
        lse_ref[0, rows, :] = top + jnp.log(total)
        if b < blocks - 1:
            nxt = base + n
            if b:
                moved = dot1(p_ref[0, b], hist_ref[0, :, pl.ds(base, n)], NN)
                hist_ref[0, :, pl.ds(nxt, n)] = moved.astype(bf16)
            hist_ref[0, :, pl.ds(nxt + n, BLK)] = kct[b]
            base = nxt


def bwd_body(q_ref, k_ref, v_ref, w_ref, tail_ref, bias_ref, tap_ref, link_ref, segc_ref, segr_ref,
             lse_ref, u_ref, gram_ref, tinv_ref, tr_ref, qt_ref, p_ref, sd_ref, hist_ref, do_ref,
             dproj_ref, dbias_ref, dtap_ref,
             dkc, dvt, dz, du, bl, *, group, heads):
    head = pl.program_id(0)
    length = q_ref.shape[0]
    blocks = length // BLK
    scale = HEADW ** -0.5
    r, c = iota2(BLK, BLK)
    bl[...] = pick_logit(tail_ref, bias_ref, head)
    lane = lax.broadcasted_iota(jnp.int32, (1, HEADW), 1)

    @pl.when(head == 0)
    def _():
        dproj_ref[:, 4 * heads * HEADW :] = jnp.zeros((length, HEADW), bf16)
        dbias_ref[...] = jnp.zeros_like(dbias_ref)

    dkc[...] = jnp.zeros_like(dkc)
    dvt[...] = jnp.zeros_like(dvt)
    base = sum(range(blocks - 1)) * BLK
    for b in reversed(range(blocks)):
        n = b * BLK
        rows = pl.ds(n, BLK)
        lse = lse_ref[0, rows, :]
        same = segc_ref[rows, :] == segr_ref[b]
        pd = jnp.exp(jnp.where(same & (r >= c), sd_ref[0, b] * scale, -1e30) - lse)
        do = do_ref[rows, :]
        dob = do.astype(bf16)
        dot_t = do.T.astype(bf16)
        dpd = dot1(dob, v_ref[rows, :].astype(bf16), NT)
        delta = jnp.sum(pd * dpd, axis=1, keepdims=True)
        if b:
            kc = hist_ref[0, :, pl.ds(base, n)]
            off = dot1(qt_ref[0, b], kc, NN) * scale - lse
            pieces = []
            for j in range(b):
                link = segc_ref[rows, :] == segr_ref[j]
                pieces.append(jnp.where(link, off[:, j * BLK : (j + 1) * BLK], -1e30))
            po = jnp.exp(jnp.concatenate(pieces, axis=1))
            dpo = dot1(dob, v_ref[pl.ds(0, n), :].astype(bf16), NT)
            delta = delta + jnp.sum(po * dpo, axis=1, keepdims=True)
            go = (po * (dpo - delta) * scale).astype(bf16)
            dvt[:, pl.ds(0, n)] += dot1(dot_t, po.astype(bf16), NN)
        dvt[:, rows] += dot1(dot_t, pd.astype(bf16), NN)
        dz[b, 0:BLK, BLK:] = pd * (dpd - delta) * scale
        dz[b, BLK:, BLK:] = dkc[:, rows]
        if b:
            dz[b, 0:BLK, 0:BLK] = dot1(go, kc, NT)
            old = dkc[:, pl.ds(0, n)].astype(bf16)
            dz[b, BLK:, 0:BLK] = dot1(old, kc, NT)
            qtt = qt_ref[0, b].astype(f32).T.astype(bf16)
            dkc[:, pl.ds(0, n)] = dot1(p_ref[0, b], old, TN) + dot1(qtt, go, NN)
            base -= (b - 1) * BLK
        else:
            dz[b, 0:BLK, 0:BLK] = jnp.zeros((BLK, BLK), f32)
            dz[b, BLK:, 0:BLK] = jnp.zeros((BLK, BLK), f32)

    col = lambda part: pl.ds(pl.multiple_of((4 * head + part) * HEADW, HEADW), HEADW)

    def phase2(g, _):
        rows = pl.ds(pl.multiple_of(g * group * BLK, BLK), group * BLK)
        blk = pl.ds(g * group, group)
        three = lambda x: x.reshape(group, BLK, x.shape[-1])
        flat = lambda x: x.reshape(group * BLK, x.shape[-1])
        u = three(u_ref[0, rows, :])
        qb = three(q_ref[rows, :]).astype(bf16)
        kb = three(k_ref[rows, :]).astype(bf16)
        sig = three(jax.nn.sigmoid(bl[rows, :]))
        beta = 2.0 * sig
        same = three(segc_ref[rows, :]) == segr_ref[blk]
        strict = same & (r > c)[None]
        upper = same & (r <= c)[None]
        gram = gram_ref[0, blk]
        s, rqt, w = gram[:, :, :BLK], gram[:, :, BLK : 2 * BLK], gram[:, :, 2 * BLK :]
        t2 = split(tinv_ref[0, blk])
        tr = tr_ref[0, blk]
        tr2 = split(tr)
        z2 = split(dz[blk])
        left2 = split(jnp.concatenate([rqt, u], axis=2))
        lti2 = split(dot3(t2, left2, TN))
        yi = dot3(lti2, z2, NN)
        r2 = jnp.concatenate([u, w], axis=2) - dot1(s.astype(bf16), tr2[0], NN)
        dbeta = -jnp.sum(yi * r2, axis=2, keepdims=True)
        dlogit = jnp.where(lane == head, flat(dbeta * beta * (1.0 - sig)), 0.0)
        tail = pl.ds(4 * heads * HEADW, HEADW)
        dproj_ref[rows, tail] = jnp.where(lane == head, dlogit.astype(bf16), dproj_ref[rows, tail])
        dbias_ref[...] += jnp.sum(dlogit, axis=0, keepdims=True)
        y = beta * yi
        dlt = -dot3(tr2, z2, NT)
        ds = jnp.where(strict, dot3(split(y), tr2, NT), 0.0)
        drqt = jnp.where(upper, dlt[:, :, :BLK], 0.0)
        dw = jnp.where(strict, -y[:, :, BLK:], 0.0)
        ub = u.astype(bf16)
        drqb, dwb, dsb = drqt.astype(bf16), dw.astype(bf16), ds.astype(bf16)
        gd = dz[blk, 0:BLK, BLK:].astype(bf16)
        du[rows, :] = flat(
            dlt[:, :, BLK:] - y[:, :, :BLK] + dot1(drqb, qb, NN) + dot1(dwb, kb, NN)
            + dot1(dsb, ub, NN) + dot1(dsb, ub, TN))
        dq = dz[blk, 0:BLK, 0:BLK] + dot1(gd, kb, NN) + dot1(drqb, ub, TN)
        dproj_ref[rows, col(0)] = flat(dq).astype(bf16)
        dk = dot1(gd, qb, TN) + dot1(dwb, ub, TN)
        dkt = dz[blk, BLK:, BLK:]
        for i in range(group):
            here = pl.ds(pl.multiple_of((g * group + i) * BLK, BLK), BLK)
            dproj_ref[here, col(1)] = (dk[i] + dkt[i].T).astype(bf16)
            dproj_ref[here, col(2)] = dvt[:, here].T.astype(bf16)
        return 0

    lax.fori_loop(0, blocks // group, phase2, 0)
    taps, link, wv = tap_ref[...], link_ref[...], w_ref[...]
    mixed = convolve(wv, taps, link)
    inv = lax.rsqrt(jnp.sum(mixed * mixed, axis=1, keepdims=True) + eps_unit)
    duv = du[...]
    dm = inv * duv - mixed * ((inv * inv * inv) * jnp.sum(duv * mixed, axis=1, keepdims=True))
    dwr = dm * taps[0:1]
    dtap_ref[0:1, :] = jnp.sum(dm * wv, axis=0, keepdims=True)
    for t in range(1, taps.shape[0]):
        dml = dm * link[:, t : t + 1]
        dwr = dwr + pltpu.roll(dml, length - t, 0) * taps[t : t + 1]
        dtap_ref[t : t + 1, :] = jnp.sum(dml * pltpu.roll(wv, t, 0), axis=0, keepdims=True)
    dproj_ref[:, col(3)] = dwr.astype(bf16)


def attn_specs(length, heads, head_of, ntap):
    blocks = length // BLK
    part = lambda p: pl.BlockSpec((length, HEADW), lambda i: (0, 4 * head_of(i) + p))
    ins = [part(0), part(1), part(2), part(3),
           pl.BlockSpec((length, HEADW), lambda i: (0, 4 * heads)),
           pl.BlockSpec((1, HEADW), lambda i: (0, 0)),
           pl.BlockSpec((ntap, HEADW), lambda i: (0, head_of(i))),
           pl.BlockSpec((length, ntap), lambda i: (0, 0)),
           pl.BlockSpec((length, 1), lambda i: (0, 0)),
           pl.BlockSpec((blocks, 1, BLK), lambda i: (0, 0, 0))]
    tri = blocks * (blocks - 1) // 2 * BLK
    shapes = [((length, 1), f32), ((length, HEADW), f32), ((blocks, BLK, 3 * BLK), f32),
              ((blocks, BLK, BLK), f32), ((blocks, BLK, 2 * BLK), f32), ((blocks, BLK, BLK), bf16),
              ((blocks, BLK, BLK), bf16), ((blocks, BLK, BLK), f32), ((BLK, tri), bf16)]
    saved = [jax.ShapeDtypeStruct((heads,) + s, d) for s, d in shapes]
    saved_specs = [
        pl.BlockSpec((1,) + s, (lambda i: (head_of(i), 0, 0)) if len(s) == 2 else (lambda i: (head_of(i), 0, 0, 0)))
        for s, _ in shapes
    ]
    return ins, saved, saved_specs


def attn_fwd(head, proj, bias, taps, link, segc, segr, before, group=4):
    length, heads = proj.shape[0], taps.shape[1] // HEADW
    ins, saved, saved_specs = attn_specs(length, heads, lambda i: head, taps.shape[0])
    out_specs = [pl.BlockSpec((length, HEADW), lambda i: (0, head))] + saved_specs
    out_shape = [jax.ShapeDtypeStruct((length, heads * HEADW), bf16)] + saved
    count = len(ins)

    def body(*refs):
        fwd_body(*refs[:count], *refs[count + len(before) :], group=group, head=head)

    return pl.pallas_call(
        body,
        grid=(1,),
        in_specs=ins + [pl.BlockSpec(memory_space=pl.ANY)] * len(before),
        out_specs=out_specs,
        out_shape=out_shape,
        input_output_aliases={count + i: i for i in range(len(before))},
        scratch_shapes=[pltpu.VMEM((length // BLK, BLK, BLK), bf16), pltpu.VMEM((length, 1), f32)],
        compiler_params=pltpu.CompilerParams(vmem_limit_bytes=58 << 20),
        cost_estimate=pl.CostEstimate(flops=4 * 10**9, bytes_accessed=1 << 20, transcendentals=10**6),
        name="path_fwd",
    )(proj, proj, proj, proj, proj, bias, taps, link, segc, segr, *before)


def attn_bwd(proj, bias, taps, link, segc, segr, saved, d_att, group=4):
    length, heads = proj.shape[0], taps.shape[1] // HEADW
    ins, _, saved_specs = attn_specs(length, heads, lambda i: i, taps.shape[0])
    blocks = length // BLK
    width = (4 * heads + 1) * HEADW
    return pl.pallas_call(
        functools.partial(bwd_body, group=group, heads=heads),
        grid=(heads,),
        in_specs=ins + saved_specs + [pl.BlockSpec((length, HEADW), lambda i: (0, i))],
        out_specs=[pl.BlockSpec((length, width), lambda i: (0, 0)),
                   pl.BlockSpec((1, HEADW), lambda i: (0, 0)),
                   pl.BlockSpec((taps.shape[0], HEADW), lambda i: (0, i))],
        out_shape=[jax.ShapeDtypeStruct((length, width), bf16),
                   jax.ShapeDtypeStruct((1, HEADW), f32),
                   jax.ShapeDtypeStruct(taps.shape, f32)],
        scratch_shapes=[pltpu.VMEM((BLK, length), f32), pltpu.VMEM((BLK, length), f32),
                        pltpu.VMEM((blocks, 2 * BLK, 2 * BLK), f32), pltpu.VMEM((length, HEADW), f32),
                        pltpu.VMEM((length, 1), f32)],
        compiler_params=pltpu.CompilerParams(vmem_limit_bytes=60 << 20),
        cost_estimate=pl.CostEstimate(flops=10**9, bytes_accessed=1 << 20, transcendentals=10**6),
        name="path_bwd",
    )(proj, proj, proj, proj, proj, bias, taps, link, segc, segr, *saved, d_att)


def place_body(shapes, columns, rows, at_ref, *refs):
    out, count = refs[len(shapes)], 0
    for source, shape, column in zip(refs, shapes, columns):
        for piece in [source] if len(shape) == 2 else [source.at[i] for i in range(shape[0])]:
            first = pl.multiple_of(at_ref[count] * rows, rows)
            out[pl.ds(first, rows), pl.ds(column, shape[-1])] = piece[...]
            count += 1


def place_rows(sources, places, columns=None, width=None):
    columns = columns or [0] * len(sources)
    width = width or sources[0].shape[-1]
    rows, kind = sources[0].shape[-2], sources[0].dtype
    total = sum(source.size for source in sources)
    size = 2 * total * kind.itemsize
    whole = lambda shape: pl.BlockSpec(shape, lambda i, at: (0,) * len(shape))
    return pl.pallas_call(
        functools.partial(place_body, [source.shape for source in sources], columns, rows),
        grid_spec=pltpu.PrefetchScalarGridSpec(
            num_scalar_prefetch=1,
            grid=(1,),
            in_specs=[whole(source.shape) for source in sources],
            out_specs=whole((total // width, width)),
        ),
        out_shape=jax.ShapeDtypeStruct((total // width, width), kind),
        compiler_params=pltpu.CompilerParams(vmem_limit_bytes=(2 * size) + (4 << 20)),
        cost_estimate=pl.CostEstimate(flops=0, bytes_accessed=size, transcendentals=0),
        name="place_rows",
    )(places, *sources)


def attn_tables(segment, ntap):
    length = segment.shape[0]
    at = jnp.arange(length, dtype=jnp.int32)
    ids = jnp.where(segment >= 0, segment, -1 - at)
    link = [jnp.ones((length,), f32)]
    for t in range(1, ntap):
        same = jnp.concatenate([jnp.zeros((t,), bool), ids[t:] == ids[:-t]])
        link.append(same.astype(f32))
    return jnp.stack(link, axis=1), ids[:, None], ids.reshape(length // BLK, 1, BLK)


def seg_ids(positions, lengths, offsets):
    inside = (positions[:, None] >= offsets[None, :]) & (
        positions[:, None] < offsets[None, :] + lengths[None, :]
    )
    number = jnp.arange(1, offsets.shape[0] + 1, dtype=jnp.int32)
    return jnp.sum(jnp.where(inside, number[None, :], 0), axis=1) - 1


def rms_scale(values):
    return lax.rsqrt(jnp.mean(values * values, axis=1, keepdims=True) + eps_norm)


def rms_back(values, gain_vec, d_normed):
    inv_rms = rms_scale(values)
    scaled = d_normed * gain_vec[None, :]
    d_values = inv_rms * scaled - values * (inv_rms * inv_rms * inv_rms) * jnp.mean(
        scaled * values, axis=1, keepdims=True
    )
    d_gain = jnp.sum(d_normed * values * inv_rms, axis=0)
    return (d_values, d_gain)


def rank_of(keys):
    return jnp.sum((keys[None, :] < keys[:, None]).astype(jnp.int32), axis=1)


def pick_rows(choice, rows):
    return jnp.dot(choice.astype(bf16), rows, preferred_element_type=f32).astype(bf16)


def exchange(rows):
    axes = ("far", "near", "tensor")
    return lax.all_to_all(rows, axes, split_axis=0, concat_axis=0, tiled=True)


def hold(*values):
    return lax.optimization_barrier(values)


def swap(rows, bit):
    size = lax.axis_size("tensor")
    return lax.ppermute(rows, "tensor", [(i, i ^ bit) for i in range(size)])


def gather_pieces(rows):
    far = swap(rows, 2)
    return rows, swap(rows, 1), far, swap(far, 1)


def to_slot(pieces, me):
    return place_rows(pieces, me ^ jnp.arange(4, dtype=jnp.int32))


def slot_piece(rows, me, other):
    size = rows.shape[0] // 4
    return lax.dynamic_slice_in_dim(rows, (me ^ other) * size, size)


def send_far(far_mate, far):
    return swap((far + swap(far_mate.astype(bf16), 1).astype(f32)).astype(bf16), 2)


def sum_group(came, mate, own):
    return own + swap(mate.astype(bf16), 1).astype(f32) + came.astype(f32)


def gather_weight(shard):
    return lax.all_gather(shard, ("far", "near"), axis=0, tiled=True)


def sum_weight(terms):
    return lax.psum_scatter(
        terms.astype(bf16), ("far", "near"), scatter_dimension=0, tiled=True
    ).astype(f32)


def to_near(rows):
    return lax.ppermute(rows, "near", [(0, 1), (1, 0)])


def to_far(rows, shift=1):
    size = lax.axis_size("far")
    return lax.ppermute(rows, "far", [(i, (i + shift) % size) for i in range(size)])


def gather_far(shard):
    return lax.all_gather(shard, "far", axis=0, tiled=False)


def far_direct(shard):
    return [to_far(shard, shift) if shift else shard for shift in range(lax.axis_size("far"))]


def both_near(mine, other, relative=False):
    size, near, far = lax.axis_size("far"), lax.axis_index("near"), lax.axis_index("far")
    spots = jnp.arange(size, dtype=jnp.int32)
    if relative:
        spots = lax.rem(far - spots + size, size)
    return place_rows(mine + other, jnp.concatenate([2 * spots + near, 2 * spots + 1 - near]))


def ring_step(held, last):
    return to_near(held), None if last else to_far(held)


def reduce_ring(parts):
    size, far, near = lax.axis_size("far"), lax.axis_index("far"), lax.axis_index("near")
    rows = parts[0].shape[0] // (2 * size)

    def share(place):
        return jnp.concatenate(
            [lax.dynamic_slice_in_dim(part, place * rows, rows) for part in parts], axis=1
        )

    held = None
    for step in range(size):
        place = lax.rem(far - 1 - step + 2 * size, size) * 2
        total = share(place + near).astype(f32) + to_near(share(place + 1 - near)).astype(f32)
        if held is not None:
            total = total + held.astype(f32)
        total = yield total
        if step < size - 1:
            held = to_far(total.astype(bf16))


def sum_far_first(terms):
    near = lax.axis_index("near")
    rows = lax.psum_scatter(terms.astype(bf16), "far", scatter_dimension=0, tiled=True)
    half = rows.shape[0] // 2
    take = lambda at: lax.dynamic_slice_in_dim(rows, at * half, half, axis=0)
    return take(near), take(1 - near)


def split_near(terms):
    size, near = lax.axis_size("far"), lax.axis_index("near")
    view = terms.astype(bf16).reshape(size, 2, -1, terms.shape[1])
    take = lambda at: lax.dynamic_slice_in_dim(view, at, 1, axis=1)[:, 0]
    return take(near), take(1 - near)


def add(mine, got):
    return (mine.astype(f32) + got.astype(f32)).astype(bf16)


def sum_far(terms):
    rows = terms.astype(bf16).reshape(-1, terms.shape[-1])
    return lax.psum_scatter(rows, "far", scatter_dimension=0, tiled=True).astype(f32)


def sum_all(part):
    part = part + to_near(part)
    for axis in ("tensor", "far"):
        size, bit = lax.axis_size(axis), 1
        while bit < size:
            part = part + lax.ppermute(part, axis, [(i, i ^ bit) for i in range(size)])
            bit *= 2
    return part


def dot(a, b, dims=NN):
    return lax.dot_general(a, b, dims, preferred_element_type=f32)


def shards(
    tokens, cotangent, w_in, w_beta, beta_bias, kernel, w_out, gain_attn, gain_ffn,
    w_gate, w_up, w_down, lengths, offsets, permutation, inverse,
):
    row_count = tokens.shape[0]
    me = lax.axis_index("tensor")
    group_rows = row_count * lax.axis_size("tensor")
    assert group_rows == SLOT and lax.axis_size("tensor") == 4
    heads = w_beta.shape[1]
    feats = w_in.shape[2]
    hidden_units = w_gate.shape[1]
    shard_rows = w_in.shape[0]
    at = jnp.arange(row_count, dtype=jnp.int32)

    send = rank_of(inverse)[None, :] == at[:, None]
    place = rank_of((permutation // row_count) * row_count + at)[:, None] == at[None, :]
    sent = pick_rows(send, tokens)
    narrow = jnp.pad(w_beta, ((0, 0), (0, HEADW - heads)))
    by_head = w_in.reshape(shard_rows, 4, heads, HEADW).transpose(0, 2, 1, 3)
    held = jnp.concatenate([by_head.reshape(shard_rows, 4 * feats), narrow], axis=1)
    size = lax.axis_size("far")
    cut, width = held.shape[1] // (2 * HEADW) * HEADW, held.shape[1]
    in_first = gather_weight(held[:, :cut])
    held = held[:, cut:]
    pieces = []

    def hop(held, last=False):
        twin, later = ring_step(held, last)
        pieces.append((held, twin))
        return later

    arrived = exchange(sent)
    for _ in range(size // 2):
        held = hop(held)
    arrived, held = hold(arrived, held)
    for _ in range(size // 2, size - 1):
        held = hop(held)
    hop(held, True)
    dealt = pick_rows(place, arrived).astype(f32)

    positions = (
        (lax.axis_index("far") * 2 + lax.axis_index("near")) * group_rows
        + jnp.arange(group_rows, dtype=jnp.int32)
    )
    tables = attn_tables(seg_ids(positions, lengths, offsets), kernel.shape[0])
    bias_local = lax.dynamic_slice_in_dim(beta_bias, me * heads, heads)
    bias_row = jnp.pad(bias_local, (0, HEADW - heads))[None, :]
    taps = lax.dynamic_slice_in_dim(kernel, me * feats, feats, axis=1)

    normed = (dealt * rms_scale(dealt) * gain_attn[None, :]).astype(bf16)
    far = swap(normed, 2)
    in_first, w_gate, w_out = hold(in_first, w_gate, w_out.T)
    gate_far = gather_far(w_gate)
    normed_all = to_slot((normed, swap(normed, 1), far, swap(far, 1)), me)
    spots = jnp.arange(size, dtype=jnp.int32)
    spots, near = 2 * lax.rem(lax.axis_index("far") - spots + size, size), lax.axis_index("near")
    full_in = place_rows(
        [in_first.reshape(2 * size, shard_rows, cut)] + [p[0] for p in pieces] + [p[1] for p in pieces],
        jnp.concatenate([jnp.arange(2 * size, dtype=jnp.int32), spots + near, spots + 1 - near]),
        [0] + [cut] * (2 * size), width,
    )
    projected = dot(normed_all, full_in)
    out_far = far_direct(w_out)
    attended, *saved = attn_fwd(0, projected, bias_row, taps, *tables, ())
    attended, *out_far = hold(attended, *out_far)
    out_twin = to_near(jnp.concatenate(out_far))
    attended, *saved = attn_fwd(1, projected, bias_row, taps, *tables, [attended] + saved)
    attended, gate_far, w_up = hold(attended, gate_far, w_up)
    gate_twin = to_near(gate_far)
    up_far = gather_far(w_up)
    for head in range(2, heads):
        attended, *saved = attn_fwd(head, projected, bias_row, taps, *tables, [attended] + saved)
    attended, out_twin, w_down = hold(attended, out_twin, w_down.T)
    down_far = gather_far(w_down)
    full_out = both_near(out_far, [out_twin.reshape((size,) + w_out.shape)], relative=True)

    att = [slot_piece(attended, me, other) for other in range(4)]
    term = lambda other: dot(att[other], full_out, NT)
    arrived_cot = exchange(pick_rows(send, cotangent))
    came, up_far, gate_twin = hold(send_far(term(3), term(2)), up_far, gate_twin)
    up_twin = to_near(up_far)
    middle = dealt + sum_group(came, term(1), term(0))
    normed2 = (middle * rms_scale(middle) * gain_ffn[None, :]).astype(bf16)
    far, mate = swap(normed2, 2), swap(normed2, 1)
    near_rows = jnp.concatenate([normed2, mate])
    full_gate = both_near([gate_far], [gate_twin])
    gate_near = dot(near_rows, full_gate)
    far, arrived_cot, up_twin, down_far, gate_near = hold(far, arrived_cot, up_twin, down_far, gate_near)
    down_twin = to_near(down_far)
    full_up = both_near([up_far], [up_twin])
    dealt_cot = pick_rows(place, arrived_cot)
    cot_near = jnp.concatenate([dealt_cot, swap(dealt_cot, 1)])
    cot_far = swap(dealt_cot, 2)
    far_rows = jnp.concatenate([far, swap(far, 1)])

    def forward(rows, gate_value):
        up_value = dot(rows, full_up)
        sig_gate = jax.nn.sigmoid(gate_value)
        return gate_value, up_value, sig_gate, (gate_value * sig_gate * up_value).astype(bf16)

    near_act, far_act = forward(near_rows, gate_near), forward(far_rows, dot(far_rows, full_gate))
    hidden_far, down_twin = hold(far_act[3], down_twin)
    full_down = both_near([down_far], [down_twin])
    cot_far = jnp.concatenate([cot_far, swap(cot_far, 1)])

    def backward(cot, act):
        gate_value, up_value, sig_gate, _ = act
        d_hidden = dot(cot, full_down)
        d_gate = d_hidden * up_value * sig_gate * (1.0 + gate_value * (1.0 - sig_gate))
        d_up = d_hidden * gate_value * sig_gate
        d_gate, d_up = d_gate.astype(bf16), d_up.astype(bf16)
        return d_gate, d_up, dot(d_gate, full_gate, NT) + dot(d_up, full_up, NT)

    d_gate_far, d_up_far, far_terms = backward(cot_far, far_act)
    far_sum = far_terms[:row_count] + swap(far_terms[row_count:].astype(bf16), 1).astype(f32)
    far_sum, cot_near, d_gate_far = hold(far_sum.astype(bf16), cot_near, d_gate_far)
    came = swap(far_sum, 2)
    d_gate_near, d_up_near, near_terms = backward(cot_near, near_act)
    join = lambda left, right: jnp.concatenate([left, right], axis=0)
    hidden, cot_rows, ffn_rows = join(near_act[3], hidden_far), join(cot_near, cot_far), join(near_rows, far_rows)
    d_wide = jnp.concatenate(
        [join(d_gate_near, d_gate_far), join(d_up_near, d_up_far)], axis=1
    )
    grad_wide = dot(ffn_rows, d_wide, TN).astype(bf16)
    ring = reduce_ring((grad_wide,))
    total = next(ring)
    grad_down = dot(cot_rows, hidden, TN).astype(bf16)
    came, grad_wide, grad_down = hold(came, grad_wide, grad_down)
    sum_down = sum_weight(grad_down)
    d_normed2 = sum_group(came, near_terms[row_count:], near_terms[:row_count])
    d_from_ffn, d_gain_ffn = rms_back(middle, gain_ffn, d_normed2)
    d_middle = dealt_cot.astype(f32) + d_from_ffn

    branch = d_middle.astype(bf16)
    far = swap(branch, 2)
    ffn_terms = dot(hidden, full_down, NT)
    far, ffn_terms = hold(far, ffn_terms)
    branch = (branch, swap(branch, 1), far, swap(far, 1))
    d_attended = to_slot([dot(piece, full_out) for piece in branch], me)
    grad_out = dot(jnp.concatenate(branch), jnp.concatenate(att), TN).astype(bf16)
    d_attended, ffn_terms, grad_out, total = hold(d_attended, ffn_terms, grad_out, total)
    total = ring.send(total)
    ffn_came = send_far(ffn_terms[3 * row_count :], ffn_terms[2 * row_count : 3 * row_count])
    d_projected, d_bias, d_taps = attn_bwd(projected, bias_row, taps, *tables, saved, d_attended)
    d_projected, ffn_came, total = hold(d_projected, ffn_came, total)
    total = ring.send(total)
    term_of = lambda other: dot(slot_piece(d_projected, me, other), full_in, NT)
    term = [None, None, term_of(2), term_of(3)]
    near_sum = term[2] + swap(term[3].astype(bf16), 1).astype(f32)
    near_sum, d_projected, middle, ffn_came = hold(near_sum.astype(bf16), d_projected, middle, ffn_came)
    came = swap(near_sum, 2)
    output = (middle + sum_group(ffn_came, ffn_terms[row_count : 2 * row_count], ffn_terms[:row_count])).astype(bf16)
    back = rank_of(permutation)[None, :] == at[:, None]
    home = rank_of((inverse // row_count) * row_count + at)[:, None] == at[None, :]
    grad_in = dot(normed_all, d_projected, TN).astype(bf16)
    grad_in, d_projected = hold(grad_in, d_projected)
    term[0], term[1] = term_of(0), term_of(1)
    d_gain_attn = (
        sum(jnp.sum(t * slot_piece(normed_all, me, o).astype(f32), axis=0) for o, t in enumerate(term))
        / gain_attn
    )
    part = grad_in.shape[1] // (2 * HEADW) * HEADW
    sum_in = sum_weight(jnp.concatenate([grad_in[:, :part], grad_out], axis=1))
    ring_in = reduce_ring((grad_in[:, part:],))
    total_in = next(ring_in)
    d_normed = sum_group(came, term[1], term[0])
    d_first, _ = rms_back(dealt, gain_attn, d_normed)
    d_input = (d_middle + d_first).astype(bf16)
    grad_sent, total, total_in = hold(pick_rows(back, d_input), total, total_in)
    peers = 2 * size * lax.axis_size("tensor")
    by_peer = lambda rows: rows.reshape(peers, -1, rows.shape[1])
    arrived = exchange(
        jnp.concatenate([by_peer(pick_rows(back, output)), by_peer(grad_sent)], axis=1)
    )
    for step in range(3, size):
        total = ring.send(total)
    total_in = ring_in.send(total_in)
    sum_wide, total_in = hold(total, total_in)
    for step in range(2, size - 1):
        total_in = ring_in.send(total_in)
    total_in = ring_in.send(total_in)
    arrived, sum_in = hold(arrived, sum_in)
    per = arrived.shape[1] // 2
    out_arrived = arrived[:, :per].reshape(row_count, -1)
    grad_arrived = arrived[:, per:].reshape(row_count, -1)

    tap_terms = lax.dynamic_update_slice_in_dim(
        jnp.zeros(kernel.shape, f32), d_taps, me * feats, axis=1
    )
    bias_terms = lax.dynamic_update_slice_in_dim(
        jnp.zeros((1, kernel.shape[1]), f32), d_bias[:, :heads], me * heads, axis=1
    )
    small = sum_all(
        jnp.concatenate([tap_terms, bias_terms, d_gain_ffn[None, :], d_gain_attn[None, :]], axis=0)
    )
    tap_count = kernel.shape[0]
    sum_in, sum_out = jnp.concatenate([sum_in[:, :part], total_in], axis=1), sum_in[:, part:].T

    out_rows = pick_rows(home, out_arrived)
    grad_rows = pick_rows(home, grad_arrived)
    in_rows = sum_in[:, : 4 * feats].reshape(shard_rows, heads, 4, HEADW).transpose(0, 2, 1, 3)
    return (
        out_rows,
        grad_rows,
        in_rows.reshape(shard_rows, 4, feats),
        sum_in[:, 4 * feats : 4 * feats + heads],
        small[tap_count, : beta_bias.shape[0]],
        small[:tap_count],
        sum_out,
        small[tap_count + 2],
        small[tap_count + 1],
        sum_wide[:, :hidden_units],
        sum_wide[:, hidden_units:],
        sum_down.T,
    )


def solution(mesh):
    shape = mesh.devices.shape
    fine = Mesh(
        mesh.devices.reshape(shape[0] // 2, 2, shape[1]), ("far", "near", "tensor")
    )
    dp = ("far", "near")
    both, rows = P(("far", "near", "tensor")), P(("far", "near", "tensor"), None)
    in_specs = (
        rows, rows, P(dp, None, "tensor"), P(dp, "tensor"), P(), P(), P("tensor", dp), P(), P(),
        P(dp, "tensor"), P(dp, "tensor"), P("tensor", dp), P(), P(), both, both,
    )
    out_specs = (
        rows, rows, P(dp, None, "tensor"), P(dp, "tensor"), P(), P(), P("tensor", dp), P(), P(),
        P(dp, "tensor"), P(dp, "tensor"), P("tensor", dp),
    )
    return jax.shard_map(shards, mesh=fine, in_specs=in_specs, out_specs=out_specs, check_vma=False)
```
